128 devices in a mesh: seq: 16 (over x, y), head: 8 (over z, core).
Axes of the slice: x: 4, y: 4, z: 4, core: 2. Of those that a mesh axis runs over, the one named last changes fastest.
Arguments:
- queries: bfloat16 [32768, 4096], P('seq', 'head'), may hold values from -24 to 24
- keys: bfloat16 [32768, 4096], P('seq', 'head'), may hold values from -24 to 24
- values: bfloat16 [32768, 4096], P('seq', 'head'), may hold values from -6 to 6
- doc_bounds: int32 [2, 32768], P(None, 'seq'), may hold values from 0 to 32768, as said below
- global_queries: bfloat16 [512, 4096], P(None, 'head'), may hold values from -24 to 24
- global_keys: bfloat16 [512, 4096], P(None, 'head'), may hold values from -24 to 24
- global_span: int32 [2, 512], replicated, may hold values from 0 to 32768, as said below
- global_proj: bfloat16 [4096, 4096], P(None, 'head'), may hold values from -0.09375 to 0.09375
Outputs:
- attended: bfloat16 [32768, 4096], P('seq', 'head')
The draws below stay inside these ranges and needn't reach their ends.
Inputs may be any that keep to these rules, and one draw needn't show every extreme that they name: `doc_bounds`: documents are runs of consecutive positions of 1 to 4096 tokens, one of exactly 4096, covering the slab; each token's entries bound its own document. `global_span`: each global token's entries are the bounds of one document of doc_bounds that it belongs to.
All inputs are finite; a program needn't handle non-finite values.
Results may differ from the reference program's by a relative error of at most 0.007.
Values may be sent and summed in bfloat16 or wider, within the bound.
A program may use at most 128 MiB of HBM per device.

```python
import math
import jax
import jax.numpy as jnp
from jax import lax

HEADS = 32
HD = 128
GLOBALS = 512
RADIUS = 512
TOK_DEV = 2048
TOKENS = 32768
DOC_MAX = 4096
N_SEQ = 16


def doc_layout(key):
    base = jax.random.fold_in(key, 4242)
    slots = TOKENS // (RADIUS // 2) + 2
    lengths = jax.random.randint(jax.random.fold_in(base, 1), (slots,), RADIUS // 2, DOC_MAX + 1)
    lengths = lengths.at[0].set(DOC_MAX)
    ends = jnp.minimum(jnp.cumsum(lengths), TOKENS).astype(jnp.int32)
    starts = jnp.concatenate([jnp.zeros((1,), jnp.int32), ends[:-1]])
    places = jnp.arange(TOKENS, dtype=jnp.int32)
    which = jnp.sum((ends[None, :] <= places[:, None]).astype(jnp.int32), axis=1)
    global_pos = jax.random.randint(jax.random.fold_in(base, 2), (GLOBALS,), 0, TOKENS)
    global_doc = which[global_pos]
    return (starts[which], ends[which], starts[global_doc], ends[global_doc])


def base_rows(key, salt, count):
    stream = jax.random.fold_in(key, salt)
    return jax.random.truncated_normal(jax.random.fold_in(stream, 3), -6.0, 6.0, (count, HEADS * HD), jnp.float32)


def draw_queries(key, part):
    rows = base_rows(key, 11, TOKENS)
    return rows.astype(jnp.bfloat16)


def draw_keys(key, part):
    rows = base_rows(key, 12, TOKENS)
    return rows.astype(jnp.bfloat16)


def draw_global_queries(key, part):
    rows = base_rows(key, 13, GLOBALS)
    return rows.astype(jnp.bfloat16)


def draw_global_keys(key, part):
    rows = base_rows(key, 14, GLOBALS)
    return rows.astype(jnp.bfloat16)


def draw_doc_bounds(key, part):
    token_start, token_end, span_start, span_end = doc_layout(key)
    return jnp.stack([token_start, token_end]).astype(jnp.int32)


def draw_global_span(key, part):
    token_start, token_end, span_start, span_end = doc_layout(key)
    return jnp.stack([span_start, span_end]).astype(jnp.int32)


def block_scale(key, dims, cuts, least, largest):
    gain = 1.0
    for axis_at, shards_of in cuts:
        steps = jax.random.uniform(jax.random.fold_in(jax.random.fold_in(key, 6), axis_at), (shards_of,), jnp.float32, least / len(cuts), largest / len(cuts))
        gain = gain * jnp.repeat(jnp.exp(steps), dims[axis_at] // shards_of).reshape((-1,) + (1,) * (len(dims) - 1 - axis_at))
    return gain


def centred(key, extent, spread, reach, cuts=(), held_as=jnp.bfloat16):
    values = spread * jax.random.normal(key, extent, jnp.float32)
    if cuts:
        values = values * block_scale(key, extent, cuts, -0.22, 0.18)
    return jnp.clip(values, -reach, reach).astype(held_as)


def setup_inputs(seed: int = 0) -> dict:
    key_of = jax.random.split(jax.random.key(seed), 9)
    return {
        "queries": draw_queries(jax.random.fold_in(key_of[8], 71), 0),
        "keys": draw_keys(jax.random.fold_in(key_of[8], 71), 0),
        "values": centred(key_of[2], (TOKENS, HEADS * HD), 1.0, 6.0, ((0, 16), (1, 8))),
        "doc_bounds": draw_doc_bounds(jax.random.fold_in(key_of[8], 71), 0),
        "global_queries": draw_global_queries(jax.random.fold_in(key_of[8], 71), 0),
        "global_keys": draw_global_keys(jax.random.fold_in(key_of[8], 71), 0),
        "global_span": draw_global_span(jax.random.fold_in(key_of[8], 71), 0),
        "global_proj": centred(key_of[7], (HEADS * HD, HEADS * HD), (HEADS * HD) ** -0.5, 0.09375, ((1, 8),)),
    }


EXCLUDED = -1e+30

def global_section(global_queries, keys, values, global_span):
    score_scale = 1.0 / math.sqrt(HD)
    positions = jnp.arange(TOKENS, dtype=jnp.int32)
    inside = (positions[None, :] >= global_span[0][:, None]) & (positions[None, :] < global_span[1][:, None])
    inside = inside.reshape(GLOBALS, N_SEQ, TOK_DEV)

    def per_head(head_index):
        query_cols = lax.dynamic_slice_in_dim(global_queries, head_index * HD, HD, 1)
        key_cols = lax.dynamic_slice_in_dim(keys, head_index * HD, HD, 1)
        value_cols = lax.dynamic_slice_in_dim(values, head_index * HD, HD, 1)
        scores = jnp.dot(query_cols, key_cols.T, preferred_element_type=jnp.float32) * score_scale
        scores = scores.reshape(GLOBALS, N_SEQ, TOK_DEV)
        masked = jnp.where(inside, scores, EXCLUDED)
        slab_peak = lax.optimization_barrier(jnp.max(masked, axis=2))
        slab_exp = jnp.where(inside, jnp.exp(masked - slab_peak[:, :, None]), 0.0)
        slab_total = lax.optimization_barrier(jnp.sum(slab_exp, axis=2))
        rounded = lax.optimization_barrier(slab_exp.astype(jnp.bfloat16)).astype(jnp.float32)
        value_slabs = value_cols.astype(jnp.float32).reshape(N_SEQ, TOK_DEV, HD)
        slab_sum = jnp.einsum('gnt,ntd->gnd', rounded, value_slabs)
        best_peak = lax.optimization_barrier(jnp.max(slab_peak, axis=1))
        factor = jnp.exp(slab_peak - best_peak[:, None])
        out_total = lax.optimization_barrier(jnp.sum(slab_total * factor, axis=1))
        out_sum = lax.optimization_barrier(jnp.sum(slab_sum * factor[:, :, None], axis=1))
        return (out_sum / out_total[:, None]).astype(jnp.bfloat16)
    per_heads = lax.map(per_head, jnp.arange(HEADS, dtype=jnp.int32))
    return jnp.transpose(per_heads, (1, 0, 2)).reshape(GLOBALS, HEADS * HD)

def token_section(queries, keys, values, doc_bounds, global_keys, global_values):
    score_scale = 1.0 / math.sqrt(HD)
    border = jnp.zeros((RADIUS, HEADS * HD), keys.dtype)
    key_padded = jnp.concatenate([border, keys, border], axis=0)
    value_padded = jnp.concatenate([border, values, border], axis=0)
    glob_keys = global_keys.astype(jnp.float32).reshape(GLOBALS, HEADS, HD)
    glob_values = global_values.astype(jnp.float32).reshape(GLOBALS, HEADS, HD)

    def one_block(block_index):
        block_start = block_index * RADIUS
        query_block = lax.dynamic_slice_in_dim(queries, block_start, RADIUS, 0).astype(jnp.float32).reshape(RADIUS, HEADS, HD)
        key_block = lax.dynamic_slice_in_dim(key_padded, block_start, 3 * RADIUS, 0).astype(jnp.float32).reshape(3 * RADIUS, HEADS, HD)
        value_block = lax.dynamic_slice_in_dim(value_padded, block_start, 3 * RADIUS, 0).astype(jnp.float32).reshape(3 * RADIUS, HEADS, HD)
        query_pos = block_start + jnp.arange(RADIUS, dtype=jnp.int32)
        key_pos = block_start - RADIUS + jnp.arange(3 * RADIUS, dtype=jnp.int32)
        doc_start = lax.dynamic_slice_in_dim(doc_bounds[0], block_start, RADIUS, 0)
        doc_end = lax.dynamic_slice_in_dim(doc_bounds[1], block_start, RADIUS, 0)
        admit = (key_pos[None, :] >= doc_start[:, None]) & (key_pos[None, :] < doc_end[:, None])
        admit = admit & (jnp.abs(key_pos[None, :] - query_pos[:, None]) <= RADIUS)
        local_scores = jnp.einsum('qhd,khd->hqk', query_block, key_block) * score_scale
        edge_scores = jnp.einsum('qhd,ghd->hqg', query_block, glob_keys) * score_scale
        masked = jnp.where(admit[None], local_scores, EXCLUDED)
        best_peak = jnp.maximum(lax.optimization_barrier(jnp.max(masked, axis=2)), lax.optimization_barrier(jnp.max(edge_scores, axis=2)))
        local_exp = jnp.where(admit[None], jnp.exp(masked - best_peak[:, :, None]), 0.0)
        edge_exp = jnp.exp(edge_scores - best_peak[:, :, None])
        total_exp = lax.optimization_barrier(jnp.sum(local_exp, axis=2)) + lax.optimization_barrier(jnp.sum(edge_exp, axis=2))
        local_weights = lax.optimization_barrier((local_exp / total_exp[:, :, None]).astype(jnp.bfloat16)).astype(jnp.float32)
        edge_weights = lax.optimization_barrier((edge_exp / total_exp[:, :, None]).astype(jnp.bfloat16)).astype(jnp.float32)
        result = jnp.einsum('hqk,khd->qhd', local_weights, value_block) + jnp.einsum('hqg,ghd->qhd', edge_weights, glob_values)
        return result.reshape(RADIUS, HEADS * HD).astype(jnp.bfloat16)
    blocks = lax.map(one_block, jnp.arange(TOKENS // RADIUS, dtype=jnp.int32))
    return blocks.reshape(TOKENS, HEADS * HD)

def reference(queries, keys, values, doc_bounds, global_queries, global_keys, global_span, global_proj):
    global_out = global_section(global_queries, keys, values, global_span)
    widened = global_out.astype(jnp.float32)
    mean_square = lax.optimization_barrier(jnp.mean(widened * widened, axis=1, keepdims=True)) + 1e-06
    inverse_root = lax.rsqrt(mean_square)
    normed = (widened * inverse_root).astype(jnp.bfloat16)
    global_values = jnp.dot(normed, global_proj, preferred_element_type=jnp.float32).astype(jnp.bfloat16)
    return token_section(queries, keys, values, doc_bounds, global_keys, global_values)
```

```python
import functools
import math

import jax
import jax.numpy as jnp
from jax import lax
from jax.experimental import pallas as pl
from jax.experimental.pallas import tpu as pltpu
from jax.sharding import PartitionSpec as P

HD = 128
RADIUS = 512
HERE = 4
TOK = 2048
GLOB = 512
WIDTH = HERE * HD
TILE = 256
SPAN = TILE + 2 * RADIUS
EXCLUDED = -1e30
LOG2_SCALE = math.log2(math.e) / math.sqrt(HD)
NX = 4
NY = 4
NHEAD = 8
XB = GLOB // NX
YB = XB // NY
MSG = WIDTH + 128
MESH = pl.DeviceIdType.MESH
F32 = jnp.float32
BF16 = jnp.bfloat16


def dot_nt(a, b):
    return lax.dot_general(a, b, (((1,), (1,)), ((), ())), preferred_element_type=F32)


def dot_nn(a, b):
    return jnp.dot(a, b, preferred_element_type=F32)


def twice(k):
    return jnp.concatenate([k, k], axis=1)


def with_ones(v):
    return jnp.concatenate([v, jnp.ones_like(v)], axis=1)


def scaled_parts(q):
    scaled = q.astype(F32) * LOG2_SCALE
    high = scaled.astype(BF16)
    low = (scaled - high.astype(F32)).astype(BF16)
    return jnp.concatenate([high, low], axis=1)


def as_column(row, count):
    return jnp.transpose(jnp.broadcast_to(row.astype(F32), (128, count)))


def combine(parts, rows):
    lane = lax.broadcasted_iota(jnp.int32, (rows, 128), 1)
    stats = [p[:, WIDTH:MSG].astype(F32) for p in parts]
    outs, logs = [], []
    for h in range(HERE):
        mine = (lane >= 3 * h) & (lane < 3 * h + 3)
        lse = [jnp.sum(jnp.where(mine, s, 0.0), axis=1, keepdims=True) for s in stats]
        top = functools.reduce(jnp.maximum, lse)
        weights = [jnp.exp2(x - top) for x in lse]
        total = functools.reduce(jnp.add, weights)
        cols = slice(h * HD, (h + 1) * HD)
        acc = functools.reduce(
            jnp.add, [w * p[:, cols].astype(F32) for w, p in zip(weights, parts)]
        )
        outs.append(acc / total)
        logs.append(top + jnp.log2(total))
    return outs, logs


def put_log(stat, h, log, lane):
    high = log.astype(BF16).astype(F32)
    mid = (log - high).astype(BF16).astype(F32)
    low = log - high - mid
    stat = jnp.where(lane == 3 * h, high, stat)
    stat = jnp.where(lane == 3 * h + 1, mid, stat)
    return jnp.where(lane == 3 * h + 2, low, stat)


def exchange_kernel(
    k_hbm, v_hbm, gq_ref, span_ref, proj_hbm,
    kl_hbm, kr_hbm, vl_hbm, vr_hbm, gv_ref,
    kbuf, vbuf, proj, bias, msg, msg_x, msg2, msg_y, gall,
    load_sems, halo_send, halo_recv, x_send, x_recv, y_send, y_recv,
    z_send, z_recv, gy_send, gy_recv, gx_send, gx_recv,
):
    seq = lax.axis_index("seq")
    head = lax.axis_index("head")
    x, y = seq // NY, seq % NY

    loads = [
        pltpu.make_async_copy(k_hbm, kbuf, load_sems.at[0]),
        pltpu.make_async_copy(v_hbm, vbuf, load_sems.at[1]),
        pltpu.make_async_copy(proj_hbm, proj, load_sems.at[2]),
    ]
    for c in loads:
        c.start()

    right = ((seq + 1) % (NX * NY), head)
    left = ((seq + NX * NY - 1) % (NX * NY), head)
    x_peers = [(((x + d) % NX) * NY + y, head) for d in range(1, NX)]
    y_peers = [(x * NY + (y + d) % NY, head) for d in range(1, NY)]
    z_peers = [(seq, (head + d) % NHEAD) for d in range(1, NHEAD)]
    everyone = [left, right] + x_peers + y_peers + z_peers
    barrier = pltpu.get_barrier_semaphore()
    for peer in everyone:
        pl.semaphore_signal(barrier, inc=1, device_id=peer, device_id_type=MESH)
    pl.semaphore_wait(barrier, len(everyone))

    def remote(src, dst, send, recv, peer):
        return pltpu.make_async_remote_copy(
            src_ref=src, dst_ref=dst, send_sem=send, recv_sem=recv,
            device_id=peer, device_id_type=MESH,
        )

    tail, head_rows = pl.ds(TOK - RADIUS, RADIUS), pl.ds(0, RADIUS)
    halos = [
        remote(k_hbm.at[tail], kl_hbm, halo_send.at[0], halo_recv.at[0], right),
        remote(k_hbm.at[head_rows], kr_hbm, halo_send.at[1], halo_recv.at[1], left),
        remote(v_hbm.at[tail], vl_hbm, halo_send.at[2], halo_recv.at[2], right),
        remote(v_hbm.at[head_rows], vr_hbm, halo_send.at[3], halo_recv.at[3], left),
    ]
    for c in halos:
        c.start()

    offset = (seq * TOK).astype(F32)
    first = as_column(span_ref[0:1, :], GLOB) - offset
    after = as_column(span_ref[1:2, :], GLOB) - offset
    lane_f = lax.broadcasted_iota(jnp.int32, (GLOB, 128), 1).astype(F32)

    @pl.loop(0, TOK // 128)
    def _(j):
        place = lane_f + (j * 128).astype(F32)
        bias[:, pl.ds(pl.multiple_of(j * 128, 128), 128)] = jnp.where(
            (place >= first) & (place < after), 0.0, EXCLUDED
        )

    loads[0].wait()
    loads[1].wait()
    lane = lax.broadcasted_iota(jnp.int32, (GLOB, 128), 1)
    stat = jnp.zeros((GLOB, 128), F32)
    for h in range(HERE):
        cols = slice(h * HD, (h + 1) * HD)
        queries = scaled_parts(gq_ref[:, cols])
        scores = dot_nt(queries, twice(kbuf[:, cols])) + bias[...]
        peak = jnp.max(scores, axis=1, keepdims=True)
        weights = jnp.exp2(scores - peak).astype(BF16)
        acc = dot_nn(weights, with_ones(vbuf[:, cols]))
        msg[:, cols] = (acc[:, :HD] / acc[:, HD:]).astype(BF16)
        stat = put_log(stat, h, peak + jnp.log2(acc[:, HD:]), lane)
    msg[:, WIDTH:MSG] = stat.astype(BF16)

    def x_rows(b):
        return pl.ds(pl.multiple_of(b * XB, XB), XB)

    def y_rows(b):
        return pl.ds(pl.multiple_of(b * YB, YB), YB)

    x_copies = []
    for d in range(1, NX):
        x_copies.append(
            remote(
                msg.at[x_rows((x + d) % NX)], msg_x.at[d - 1],
                x_send.at[d - 1], x_recv.at[d - 1], x_peers[d - 1],
            )
        )
    for c in x_copies:
        c.start()
    for c in x_copies:
        c.wait_recv()
    outs, logs = combine(
        [msg[x_rows(x), :]] + [msg_x[d] for d in range(NX - 1)], XB
    )
    lane = lax.broadcasted_iota(jnp.int32, (XB, 128), 1)
    stat = jnp.zeros((XB, 128), F32)
    for h in range(HERE):
        msg2[:, h * HD:(h + 1) * HD] = outs[h].astype(BF16)
        stat = put_log(stat, h, logs[h], lane)
    msg2[:, WIDTH:MSG] = stat.astype(BF16)

    y_copies = []
    for d in range(1, NY):
        y_copies.append(
            remote(
                msg2.at[y_rows((y + d) % NY)], msg_y.at[d - 1],
                y_send.at[d - 1], y_recv.at[d - 1], y_peers[d - 1],
            )
        )
    for c in y_copies:
        c.start()
    for c in y_copies:
        c.wait_recv()
    outs, _ = combine([msg2[y_rows(y), :]] + [msg_y[d] for d in range(NY - 1)], YB)
    gall[head] = jnp.concatenate([o.astype(BF16) for o in outs], axis=1)

    z_copies = []
    for d in range(1, NHEAD):
        z_copies.append(
            remote(
                gall.at[head], gall.at[head],
                z_send.at[d - 1], z_recv.at[d - 1], z_peers[d - 1],
            )
        )
    for c in z_copies:
        c.start()
    for c in z_copies:
        c.wait_recv()
    squares = jnp.zeros((YB, 1), F32)
    for g in range(NHEAD):
        wide = gall[g].astype(F32)
        squares = squares + jnp.sum(wide * wide, axis=1, keepdims=True)
    inverse = lax.rsqrt(squares / (NHEAD * WIDTH) + 1e-06)
    loads[2].wait()
    total = jnp.zeros((YB, WIDTH), F32)
    for g in range(NHEAD):
        normed = (gall[g].astype(F32) * inverse).astype(BF16)
        total = total + dot_nn(normed, proj[g * WIDTH:(g + 1) * WIDTH, :])
    mine = pl.ds(pl.multiple_of(x * XB + y * YB, YB), YB)
    gv_ref[mine, :] = total.astype(BF16)

    gy_copies = []
    for d in range(1, NY):
        gy_copies.append(
            remote(
                gv_ref.at[mine], gv_ref.at[mine],
                gy_send.at[d - 1], gy_recv.at[d - 1], y_peers[d - 1],
            )
        )
    for c in gy_copies:
        c.start()
    for c in gy_copies:
        c.wait_recv()
    gx_copies = []
    for d in range(1, NX):
        gx_copies.append(
            remote(
                gv_ref.at[x_rows(x)], gv_ref.at[x_rows(x)],
                gx_send.at[d - 1], gx_recv.at[d - 1], x_peers[d - 1],
            )
        )
    for c in gx_copies:
        c.start()
    for c in gx_copies:
        c.wait_recv()
    for c in halos:
        c.wait_recv()
    for c in x_copies + y_copies + z_copies + gy_copies + gx_copies + halos:
        c.wait_send()


def exchange(keys, values, global_queries, global_span, global_proj):
    anyspec = pl.BlockSpec(memory_space=pl.ANY)
    vmem = pl.BlockSpec(memory_space=pltpu.VMEM)
    halo = jax.ShapeDtypeStruct((RADIUS, WIDTH), BF16)
    dma = pltpu.SemaphoreType.DMA
    return pl.pallas_call(
        exchange_kernel,
        out_shape=(halo,) * 4 + (jax.ShapeDtypeStruct((GLOB, WIDTH), BF16),),
        in_specs=[anyspec, anyspec, vmem, vmem, anyspec],
        out_specs=(anyspec,) * 4 + (vmem,),
        scratch_shapes=[
            pltpu.VMEM((TOK, WIDTH), BF16),
            pltpu.VMEM((TOK, WIDTH), BF16),
            pltpu.VMEM((NHEAD * WIDTH, WIDTH), BF16),
            pltpu.VMEM((GLOB, TOK), F32),
            pltpu.VMEM((GLOB, MSG), BF16),
            pltpu.VMEM((NX - 1, XB, MSG), BF16),
            pltpu.VMEM((XB, MSG), BF16),
            pltpu.VMEM((NY - 1, YB, MSG), BF16),
            pltpu.VMEM((NHEAD, YB, WIDTH), BF16),
            dma((3,)), dma((4,)), dma((4,)),
            dma((NX - 1,)), dma((NX - 1,)), dma((NY - 1,)), dma((NY - 1,)),
            dma((NHEAD - 1,)), dma((NHEAD - 1,)),
            dma((NY - 1,)), dma((NY - 1,)), dma((NX - 1,)), dma((NX - 1,)),
        ],
        compiler_params=pltpu.CompilerParams(
            collective_id=0, has_side_effects=True, vmem_limit_bytes=60 * 2**20
        ),
        name="exchange",
    )(keys, values, global_queries, global_span, global_proj)


CHUNKS = (TOK + 2 * RADIUS) // TILE
EARLY = RADIUS // TILE


def attend_kernel(
    q_ref, doc_ref, gk_ref, gv_ref, k_hbm, v_hbm, kl_hbm, kr_hbm, vl_hbm, vr_hbm,
    out_ref, kbuf, vbuf, bias, k_sems, v_sems,
):
    t = pl.program_id(0)
    seq = lax.axis_index("seq")

    def chunk(own, before, behind, buf, sems, c):
        if c < EARLY:
            src = before.at[pl.ds(c * TILE, TILE)]
        elif c < CHUNKS - EARLY:
            src = own.at[pl.ds((c - EARLY) * TILE, TILE)]
        else:
            src = behind.at[pl.ds((c - CHUNKS + EARLY) * TILE, TILE)]
        return pltpu.make_async_copy(src, buf.at[pl.ds(c * TILE, TILE)], sems.at[c])

    k_loads = [chunk(k_hbm, kl_hbm, kr_hbm, kbuf, k_sems, c) for c in range(CHUNKS)]
    v_loads = [chunk(v_hbm, vl_hbm, vr_hbm, vbuf, v_sems, c) for c in range(CHUNKS)]
    span_chunks = SPAN // TILE

    @pl.when(t == 0)
    def _():
        for c in range(CHUNKS):
            k_loads[c].start()
            v_loads[c].start()

    base = (seq * TOK - RADIUS + t * TILE).astype(F32)
    first = as_column(doc_ref[0:1, :], TILE) - base
    after = as_column(doc_ref[1:2, :], TILE) - base
    row = lax.broadcasted_iota(jnp.int32, (TILE, 128), 0).astype(F32)
    lane = lax.broadcasted_iota(jnp.int32, (TILE, 128), 1).astype(F32)
    first = jnp.maximum(first, row)
    after = jnp.minimum(after, row + (2 * RADIUS + 1))
    for j in range(SPAN // 128):
        place = lane + float(j * 128)
        bias[:, j * 128:(j + 1) * 128] = jnp.where(
            (place >= first) & (place < after), 0.0, EXCLUDED
        )

    @pl.when(t == 0)
    def _():
        for c in range(span_chunks):
            k_loads[c].wait()
            v_loads[c].wait()

    for c in range(span_chunks, CHUNKS):
        @pl.when(t == c - span_chunks + 1)
        def _(c=c):
            k_loads[c].wait()
            v_loads[c].wait()

    window = pl.ds(pl.multiple_of(t * TILE, TILE), SPAN)
    for h in range(HERE):
        cols = slice(h * HD, (h + 1) * HD)
        queries = scaled_parts(q_ref[:, cols])
        local = dot_nt(queries, twice(kbuf[window, cols])) + bias[...]
        edge = dot_nt(queries, twice(gk_ref[:, cols]))
        peak = jnp.maximum(
            jnp.max(local, axis=1, keepdims=True), jnp.max(edge, axis=1, keepdims=True)
        )
        local_exp = jnp.exp2(local - peak).astype(BF16)
        edge_exp = jnp.exp2(edge - peak).astype(BF16)
        acc = dot_nn(local_exp, with_ones(vbuf[window, cols]))
        acc = acc + dot_nn(edge_exp, with_ones(gv_ref[:, cols]))
        out_ref[:, cols] = (acc[:, :HD] / acc[:, HD:]).astype(BF16)


def attend(queries, doc_bounds, global_keys, global_values, keys, values, halos):
    anyspec = pl.BlockSpec(memory_space=pl.ANY)
    whole = pl.BlockSpec((GLOB, WIDTH), lambda t: (0, 0))
    tile = pl.BlockSpec((TILE, WIDTH), lambda t: (t, 0))
    dma = pltpu.SemaphoreType.DMA
    return pl.pallas_call(
        attend_kernel,
        out_shape=jax.ShapeDtypeStruct((TOK, WIDTH), BF16),
        grid=(TOK // TILE,),
        in_specs=[tile, pl.BlockSpec((2, TILE), lambda t: (0, t)), whole, whole]
        + [anyspec] * 6,
        out_specs=tile,
        scratch_shapes=[
            pltpu.VMEM((TOK + 2 * RADIUS, WIDTH), BF16),
            pltpu.VMEM((TOK + 2 * RADIUS, WIDTH), BF16),
            pltpu.VMEM((TILE, SPAN), F32),
            dma((CHUNKS,)), dma((CHUNKS,)),
        ],
        compiler_params=pltpu.CompilerParams(vmem_limit_bytes=60 * 2**20),
        name="attend",
    )(queries, doc_bounds, global_keys, global_values, keys, values, *halos)


def local(queries, keys, values, doc_bounds, global_queries, global_keys, global_span, global_proj):
    kl, kr, vl, vr, global_values = exchange(
        keys, values, global_queries, global_span, global_proj
    )
    return attend(
        queries, doc_bounds, global_keys, global_values, keys, values, (kl, kr, vl, vr)
    )


def solution(mesh):
    in_specs = (
        P("seq", "head"),
        P("seq", "head"),
        P("seq", "head"),
        P(None, "seq"),
        P(None, "head"),
        P(None, "head"),
        P(),
        P(None, "head"),
    )
    out_specs = P("seq", "head")
    return jax.shard_map(local, mesh=mesh, in_specs=in_specs, out_specs=out_specs, check_vma=False)
```

```python
import functools
import math

import jax
import jax.numpy as jnp
from jax import lax
from jax.experimental import pallas as pl
from jax.experimental.pallas import tpu as pltpu
from jax.sharding import PartitionSpec as P

HD = 128
RADIUS = 512
HERE = 4
TOK = 2048
GLOB = 512
WIDTH = HERE * HD
TILE = 256
SPAN = TILE + 2 * RADIUS
EXCLUDED = -1e30
LOG2_SCALE = math.log2(math.e) / math.sqrt(HD)
NX = 4
NY = 4
NHEAD = 8
XB = GLOB // NX
YB = XB // NY
PARTS = HERE + 1
MESH = pl.DeviceIdType.MESH
F32 = jnp.float32
BF16 = jnp.bfloat16


def dot_nt(a, b):
    return lax.dot_general(a, b, (((1,), (1,)), ((), ())), preferred_element_type=F32)


def dot_nn(a, b):
    return jnp.dot(a, b, preferred_element_type=F32)


def twice(k):
    return jnp.concatenate([k, k], axis=1)


def with_ones(v):
    return jnp.concatenate([v, jnp.ones_like(v)], axis=1)


def scaled_parts(q):
    scaled = q.astype(F32) * LOG2_SCALE
    high = scaled.astype(BF16)
    low = (scaled - high.astype(F32)).astype(BF16)
    return jnp.concatenate([high, low], axis=1)


def as_column(row, count):
    return jnp.transpose(jnp.broadcast_to(row.astype(F32), (128, count)))


def combine(parts, rows):
    lane = lax.broadcasted_iota(jnp.int32, (rows, 128), 1)
    stats = [p[HERE].astype(F32) for p in parts]
    outs, logs = [], []
    for h in range(HERE):
        mine = (lane >= 3 * h) & (lane < 3 * h + 3)
        lse = [jnp.sum(jnp.where(mine, s, 0.0), axis=1, keepdims=True) for s in stats]
        top = functools.reduce(jnp.maximum, lse)
        weights = [jnp.exp2(x - top) for x in lse]
        total = functools.reduce(jnp.add, weights)
        acc = functools.reduce(
            jnp.add, [w * p[h].astype(F32) for w, p in zip(weights, parts)]
        )
        outs.append(acc / total)
        logs.append(top + jnp.log2(total))
    return outs, logs


def put_log(stat, h, log, lane):
    high = log.astype(BF16).astype(F32)
    mid = (log - high).astype(BF16).astype(F32)
    low = log - high - mid
    stat = jnp.where(lane == 3 * h, high, stat)
    stat = jnp.where(lane == 3 * h + 1, mid, stat)
    return jnp.where(lane == 3 * h + 2, low, stat)


TILES = TOK // TILE


def kernel(
    gq_ref, gk_ref, span_ref, doc_ref, q_hbm, k_hbm, v_hbm, proj_hbm, out_hbm,
    qbuf, kbuf, vbuf, proj, bias, local_bias, sums, edges, obuf,
    msg, msg_x, msg2, msg_y, gall, gv,
    load_sems, out_sems, halo_send, halo_recv, x_send, x_recv, y_send, y_recv,
    z_send, z_recv, gy_send, gy_recv, gx_send, gx_recv,
):
    seq = lax.axis_index("seq")
    head = lax.axis_index("head")
    x, y = seq // NY, seq % NY
    right = ((seq + 1) % (NX * NY), head)
    left = ((seq + NX * NY - 1) % (NX * NY), head)
    x_peers = [(((x + d) % NX) * NY + y, head) for d in range(1, NX)]
    y_peers = [(x * NY + (y + d) % NY, head) for d in range(1, NY)]
    z_peers = [(seq, (head + d) % NHEAD) for d in range(1, NHEAD)]
    everyone = [left, right] + x_peers + y_peers + z_peers

    def remote(src, dst, send, recv, peer):
        return pltpu.make_async_remote_copy(
            src_ref=src, dst_ref=dst, send_sem=send, recv_sem=recv,
            device_id=peer, device_id_type=MESH,
        )

    def x_rows(b):
        return pl.ds(pl.multiple_of(b * XB, XB), XB)

    def y_rows(b):
        return pl.ds(pl.multiple_of(b * YB, YB), YB)

    own = pl.ds(RADIUS, TOK)
    loads = [
        pltpu.make_async_copy(k_hbm, kbuf.at[own], load_sems.at[0]),
        pltpu.make_async_copy(v_hbm, vbuf.at[own], load_sems.at[1]),
        pltpu.make_async_copy(q_hbm, qbuf, load_sems.at[2]),
        pltpu.make_async_copy(proj_hbm, proj, load_sems.at[3]),
    ]
    front, back = pl.ds(0, RADIUS), pl.ds(TOK - RADIUS, RADIUS)
    before, behind = pl.ds(0, RADIUS), pl.ds(TOK + RADIUS, RADIUS)
    halos = [
        remote(k_hbm.at[back], kbuf.at[before], halo_send.at[0], halo_recv.at[0], right),
        remote(k_hbm.at[front], kbuf.at[behind], halo_send.at[1], halo_recv.at[1], left),
        remote(v_hbm.at[back], vbuf.at[before], halo_send.at[2], halo_recv.at[2], right),
        remote(v_hbm.at[front], vbuf.at[behind], halo_send.at[3], halo_recv.at[3], left),
    ]

    def x_copy(d, h):
        return remote(
            msg.at[h, x_rows((x + d) % NX)], msg_x.at[d - 1, h],
            x_send.at[d - 1, h], x_recv.at[d - 1, h], x_peers[d - 1],
        )

    def y_copy(d):
        return remote(
            msg2.at[:, y_rows((y + d) % NY)], msg_y.at[d - 1],
            y_send.at[d - 1], y_recv.at[d - 1], y_peers[d - 1],
        )

    def z_copy(d):
        return remote(
            gall.at[head], gall.at[head],
            z_send.at[d - 1], z_recv.at[d - 1], z_peers[d - 1],
        )

    mine = pl.ds(pl.multiple_of(x * XB + y * YB, YB), YB)

    def gy_copy(d):
        return remote(
            gv.at[mine], gv.at[mine],
            gy_send.at[d - 1], gy_recv.at[d - 1], y_peers[d - 1],
        )

    def gx_copy(d):
        return remote(
            gv.at[x_rows(x)], gv.at[x_rows(x)],
            gx_send.at[d - 1], gx_recv.at[d - 1], x_peers[d - 1],
        )

    for c in loads:
        c.start()
    barrier = pltpu.get_barrier_semaphore()
    for peer in everyone:
        pl.semaphore_signal(barrier, inc=1, device_id=peer, device_id_type=MESH)
    pl.semaphore_wait(barrier, len(everyone))
    for c in halos:
        c.start()

    offset = (seq * TOK).astype(F32)
    span_first = as_column(span_ref[0:1, :], GLOB) - offset
    span_after = as_column(span_ref[1:2, :], GLOB) - offset
    lane_f = lax.broadcasted_iota(jnp.int32, (GLOB, 128), 1).astype(F32)

    @pl.loop(0, TOK // 128)
    def _(j):
        place = lane_f + (j * 128).astype(F32)
        bias[:, pl.ds(pl.multiple_of(j * 128, 128), 128)] = jnp.where(
            (place >= span_first) & (place < span_after), 0.0, EXCLUDED
        )

    loads[0].wait()
    loads[1].wait()
    lane = lax.broadcasted_iota(jnp.int32, (GLOB, 128), 1)
    stat = jnp.zeros((GLOB, 128), F32)
    for h in range(HERE):
        cols = slice(h * HD, (h + 1) * HD)
        queries = scaled_parts(gq_ref[:, cols])
        scores = dot_nt(queries, twice(kbuf[own, cols])) + bias[...]
        peak = jnp.max(scores, axis=1, keepdims=True)
        weights = jnp.exp2(scores - peak).astype(BF16)
        acc = dot_nn(weights, with_ones(vbuf[own, cols]))
        msg[h] = (acc[:, :HD] / acc[:, HD:]).astype(BF16)
        stat = put_log(stat, h, peak + jnp.log2(acc[:, HD:]), lane)
        for d in (2, 1, 3):
            x_copy(d, h).start()
    msg[HERE] = stat.astype(BF16)
    for d in (2, 1, 3):
        x_copy(d, HERE).start()
    loads[2].wait()

    def after_x():
        for d in range(1, NX):
            for h in range(PARTS):
                x_copy(d, h).wait_recv()
        parts = [[msg[h, x_rows(x), :] for h in range(PARTS)]]
        parts += [[msg_x[d, h] for h in range(PARTS)] for d in range(NX - 1)]
        outs, logs = combine(parts, XB)
        lane = lax.broadcasted_iota(jnp.int32, (XB, 128), 1)
        stat = jnp.zeros((XB, 128), F32)
        for h in range(HERE):
            msg2[h] = outs[h].astype(BF16)
            stat = put_log(stat, h, logs[h], lane)
        msg2[HERE] = stat.astype(BF16)
        for d in range(1, NY):
            y_copy(d).start()

    def after_y():
        for d in range(1, NY):
            y_copy(d).wait_recv()
        parts = [[msg2[h, y_rows(y), :] for h in range(PARTS)]]
        parts += [[msg_y[d, h] for h in range(PARTS)] for d in range(NY - 1)]
        outs, _ = combine(parts, YB)
        gall[head] = jnp.concatenate([o.astype(BF16) for o in outs], axis=1)
        for d in range(1, NHEAD):
            z_copy(d).start()

    def after_z():
        for d in range(1, NHEAD):
            z_copy(d).wait_recv()
        squares = jnp.zeros((YB, 1), F32)
        for g in range(NHEAD):
            wide = gall[g].astype(F32)
            squares = squares + jnp.sum(wide * wide, axis=1, keepdims=True)
        inverse = lax.rsqrt(squares / (NHEAD * WIDTH) + 1e-06)
        loads[3].wait()
        total = jnp.zeros((YB, WIDTH), F32)
        for g in range(NHEAD):
            normed = (gall[g].astype(F32) * inverse).astype(BF16)
            total = total + dot_nn(normed, proj[g * WIDTH:(g + 1) * WIDTH, :])
        gv[mine, :] = total.astype(BF16)
        for d in range(1, NY):
            gy_copy(d).start()

    def after_gy():
        for d in range(1, NY):
            gy_copy(d).wait_recv()
        for d in range(1, NX):
            gx_copy(d).start()

    @pl.loop(0, TILES)
    def _(i):
        half = TILES // 2
        inner = half // 2
        t = jnp.where(i < half, i + inner, jnp.where(i < half + inner, i - half, i))

        @pl.when(i == half)
        def _():
            for c in halos:
                c.wait_recv()

        base = (seq * TOK - RADIUS + t * TILE).astype(F32)
        here = pl.ds(pl.multiple_of(t * TILE, TILE), TILE)
        first = as_column(doc_ref[0:1, here], TILE) - base
        after = as_column(doc_ref[1:2, here], TILE) - base
        row = lax.broadcasted_iota(jnp.int32, (TILE, 128), 0).astype(F32)
        lane = lax.broadcasted_iota(jnp.int32, (TILE, 128), 1).astype(F32)
        first = jnp.maximum(first, row)
        after = jnp.minimum(after, row + (2 * RADIUS + 1))
        for j in range(SPAN // 128):
            place = lane + float(j * 128)
            local_bias[:, j * 128:(j + 1) * 128] = jnp.where(
                (place >= first) & (place < after), 0.0, EXCLUDED
            )
        window = pl.ds(pl.multiple_of(t * TILE, TILE), SPAN)
        for h in range(HERE):
            cols = slice(h * HD, (h + 1) * HD)
            queries = scaled_parts(qbuf[here, cols])
            near = dot_nt(queries, twice(kbuf[window, cols])) + local_bias[...]
            edge = dot_nt(queries, twice(gk_ref[:, cols]))
            peak = jnp.maximum(
                jnp.max(near, axis=1, keepdims=True), jnp.max(edge, axis=1, keepdims=True)
            )
            edges[t, h] = jnp.exp2(edge - peak).astype(BF16)
            near_exp = jnp.exp2(near - peak).astype(BF16)
            sums[t, h] = dot_nn(near_exp, with_ones(vbuf[window, cols]))

        for step, work in enumerate((after_x, after_y, after_z, after_gy)):
            pl.when(i == step)(work)

    for d in range(1, NX):
        gx_copy(d).wait_recv()

    def out_copy(t):
        here = pl.ds(pl.multiple_of(t * TILE, TILE), TILE)
        return pltpu.make_async_copy(obuf.at[here], out_hbm.at[here], out_sems.at[t])

    @pl.loop(0, TILES)
    def _(t):
        here = pl.ds(pl.multiple_of(t * TILE, TILE), TILE)
        for h in range(HERE):
            cols = slice(h * HD, (h + 1) * HD)
            acc = sums[t, h] + dot_nn(edges[t, h], with_ones(gv[:, cols]))
            obuf[here, cols] = (acc[:, :HD] / acc[:, HD:]).astype(BF16)
        out_copy(t).start()

    for t in range(TILES):
        out_copy(t).wait()
    for d in range(1, NX):
        for h in range(PARTS):
            x_copy(d, h).wait_send()
        gx_copy(d).wait_send()
    for d in range(1, NY):
        y_copy(d).wait_send()
        gy_copy(d).wait_send()
    for d in range(1, NHEAD):
        z_copy(d).wait_send()
    for c in halos:
        c.wait_send()


def local(queries, keys, values, doc_bounds, global_queries, global_keys, global_span, global_proj):
    anyspec = pl.BlockSpec(memory_space=pl.ANY)
    vmem = pl.BlockSpec(memory_space=pltpu.VMEM)
    dma = pltpu.SemaphoreType.DMA
    return pl.pallas_call(
        kernel,
        out_shape=jax.ShapeDtypeStruct((TOK, WIDTH), BF16),
        in_specs=[vmem] * 4 + [anyspec] * 4,
        out_specs=anyspec,
        scratch_shapes=[
            pltpu.VMEM((TOK, WIDTH), BF16),
            pltpu.VMEM((TOK + 2 * RADIUS, WIDTH), BF16),
            pltpu.VMEM((TOK + 2 * RADIUS, WIDTH), BF16),
            pltpu.VMEM((NHEAD * WIDTH, WIDTH), BF16),
            pltpu.VMEM((GLOB, TOK), F32),
            pltpu.VMEM((TILE, SPAN), F32),
            pltpu.VMEM((TILES, HERE, TILE, 2 * HD), F32),
            pltpu.VMEM((TILES, HERE, TILE, GLOB), BF16),
            pltpu.VMEM((TOK, WIDTH), BF16),
            pltpu.VMEM((PARTS, GLOB, HD), BF16),
            pltpu.VMEM((NX - 1, PARTS, XB, HD), BF16),
            pltpu.VMEM((PARTS, XB, HD), BF16),
            pltpu.VMEM((NY - 1, PARTS, YB, HD), BF16),
            pltpu.VMEM((NHEAD, YB, WIDTH), BF16),
            pltpu.VMEM((GLOB, WIDTH), BF16),
            dma((4,)), dma((TILES,)), dma((4,)), dma((4,)),
            dma((NX - 1, PARTS)), dma((NX - 1, PARTS)), dma((NY - 1,)), dma((NY - 1,)),
            dma((NHEAD - 1,)), dma((NHEAD - 1,)),
            dma((NY - 1,)), dma((NY - 1,)), dma((NX - 1,)), dma((NX - 1,)),
        ],
        compiler_params=pltpu.CompilerParams(
            collective_id=0, has_side_effects=True, vmem_limit_bytes=63 * 2**20
        ),
        name="attention",
    )(
        global_queries, global_keys, global_span, doc_bounds,
        queries, keys, values, global_proj,
    )


def solution(mesh):
    in_specs = (
        P("seq", "head"),
        P("seq", "head"),
        P("seq", "head"),
        P(None, "seq"),
        P(None, "head"),
        P(None, "head"),
        P(),
        P(None, "head"),
    )
    out_specs = P("seq", "head")
    return jax.shard_map(local, mesh=mesh, in_specs=in_specs, out_specs=out_specs, check_vma=False)
```

```python
import functools
import math

import jax
import jax.numpy as jnp
from jax import lax
from jax.experimental import pallas as pl
from jax.experimental.pallas import tpu as pltpu
from jax.sharding import PartitionSpec as P

HD = 128
RADIUS = 512
HERE = 4
TOK = 2048
GLOB = 512
WIDTH = HERE * HD
TILE = 256
SPAN = TILE + 2 * RADIUS
EXCLUDED = -1e30
LOG2_SCALE = math.log2(math.e) / math.sqrt(HD)
NX = 4
NY = 4
NHEAD = 8
XB = GLOB // NX
YB = XB // NY
PARTS = HERE + 1
MESH = pl.DeviceIdType.MESH
F32 = jnp.float32
BF16 = jnp.bfloat16


def dot_nt(a, b):
    return lax.dot_general(a, b, (((1,), (1,)), ((), ())), preferred_element_type=F32)


def dot_nn(a, b):
    return jnp.dot(a, b, preferred_element_type=F32)


def twice(k):
    return jnp.concatenate([k, k], axis=1)


def with_ones(v):
    return jnp.concatenate([v, jnp.ones_like(v)], axis=1)


def scaled_parts(q):
    scaled = q.astype(F32) * LOG2_SCALE
    high = scaled.astype(BF16)
    low = (scaled - high.astype(F32)).astype(BF16)
    return jnp.concatenate([high, low], axis=1)


def as_column(row, count):
    return jnp.transpose(jnp.broadcast_to(row.astype(F32), (128, count)))


def combine(parts, rows):
    lane = lax.broadcasted_iota(jnp.int32, (rows, 128), 1)
    stats = [p[HERE].astype(F32) for p in parts]
    outs, logs = [], []
    for h in range(HERE):
        mine = (lane >= 3 * h) & (lane < 3 * h + 3)
        lse = [jnp.sum(jnp.where(mine, s, 0.0), axis=1, keepdims=True) for s in stats]
        top = functools.reduce(jnp.maximum, lse)
        weights = [jnp.exp2(x - top) for x in lse]
        total = functools.reduce(jnp.add, weights)
        acc = functools.reduce(
            jnp.add, [w * p[h].astype(F32) for w, p in zip(weights, parts)]
        )
        outs.append(acc / total)
        logs.append(top + jnp.log2(total))
    return outs, logs


def put_log(stat, h, log, lane):
    high = log.astype(BF16).astype(F32)
    mid = (log - high).astype(BF16).astype(F32)
    low = log - high - mid
    stat = jnp.where(lane == 3 * h, high, stat)
    stat = jnp.where(lane == 3 * h + 1, mid, stat)
    return jnp.where(lane == 3 * h + 2, low, stat)


TILES = TOK // TILE


def kernel(
    gq_ref, gk_ref, span_ref, doc_ref, q_hbm, k_hbm, v_hbm, proj_hbm, out_hbm,
    qbuf, kbuf, vbuf, proj, bias, local_bias, sums, edges, factor, obuf,
    msg, msg_x, msg2, msg_y, gall, gv,
    load_sems, out_sems, halo_send, halo_recv, x_send, x_recv, y_send, y_recv,
    z_send, z_recv, gy_send, gy_recv, gx_send, gx_recv,
):
    seq = lax.axis_index("seq")
    head = lax.axis_index("head")
    x, y = seq // NY, seq % NY
    right = ((seq + 1) % (NX * NY), head)
    left = ((seq + NX * NY - 1) % (NX * NY), head)
    x_peers = [(((x + d) % NX) * NY + y, head) for d in range(1, NX)]
    y_peers = [(x * NY + (y + d) % NY, head) for d in range(1, NY)]
    z_peers = [(seq, (head + d) % NHEAD) for d in range(1, NHEAD)]
    everyone = [left, right] + x_peers + y_peers + z_peers

    def remote(src, dst, send, recv, peer):
        return pltpu.make_async_remote_copy(
            src_ref=src, dst_ref=dst, send_sem=send, recv_sem=recv,
            device_id=peer, device_id_type=MESH,
        )

    def x_rows(b):
        return pl.ds(pl.multiple_of(b * XB, XB), XB)

    def y_rows(b):
        return pl.ds(pl.multiple_of(b * YB, YB), YB)

    own = pl.ds(RADIUS, TOK)
    loads = [
        pltpu.make_async_copy(k_hbm, kbuf.at[own], load_sems.at[0]),
        pltpu.make_async_copy(v_hbm, vbuf.at[own], load_sems.at[1]),
        pltpu.make_async_copy(q_hbm, qbuf, load_sems.at[2]),
        pltpu.make_async_copy(proj_hbm, proj, load_sems.at[3]),
    ]
    front, back = pl.ds(0, RADIUS), pl.ds(TOK - RADIUS, RADIUS)
    before, behind = pl.ds(0, RADIUS), pl.ds(TOK + RADIUS, RADIUS)
    halos = [
        remote(k_hbm.at[back], kbuf.at[before], halo_send.at[0], halo_recv.at[0], right),
        remote(k_hbm.at[front], kbuf.at[behind], halo_send.at[1], halo_recv.at[1], left),
        remote(v_hbm.at[back], vbuf.at[before], halo_send.at[2], halo_recv.at[2], right),
        remote(v_hbm.at[front], vbuf.at[behind], halo_send.at[3], halo_recv.at[3], left),
    ]

    def x_copy(d, h):
        return remote(
            msg.at[h, x_rows((x + d) % NX)], msg_x.at[d - 1, h],
            x_send.at[d - 1, h], x_recv.at[d - 1, h], x_peers[d - 1],
        )

    def y_copy(d):
        return remote(
            msg2.at[:, y_rows((y + d) % NY)], msg_y.at[d - 1],
            y_send.at[d - 1], y_recv.at[d - 1], y_peers[d - 1],
        )

    def z_copy(d):
        return remote(
            gall.at[head], gall.at[head],
            z_send.at[d - 1], z_recv.at[d - 1], z_peers[d - 1],
        )

    mine = pl.ds(pl.multiple_of(x * XB + y * YB, YB), YB)

    def gy_copy(d):
        return remote(
            gv.at[mine], gv.at[mine],
            gy_send.at[d - 1], gy_recv.at[d - 1], y_peers[d - 1],
        )

    def gx_copy(d):
        return remote(
            gv.at[x_rows(x)], gv.at[x_rows(x)],
            gx_send.at[d - 1], gx_recv.at[d - 1], x_peers[d - 1],
        )

    for c in loads:
        c.start()
    barrier = pltpu.get_barrier_semaphore()
    for peer in everyone:
        pl.semaphore_signal(barrier, inc=1, device_id=peer, device_id_type=MESH)
    pl.semaphore_wait(barrier, len(everyone))
    halos[0].start()
    halos[1].start()

    offset = (seq * TOK).astype(F32)
    span_first = as_column(span_ref[0:1, :], GLOB) - offset
    span_after = as_column(span_ref[1:2, :], GLOB) - offset
    lane_f = lax.broadcasted_iota(jnp.int32, (GLOB, 128), 1).astype(F32)

    @pl.loop(0, TOK // 128)
    def _(j):
        place = lane_f + (j * 128).astype(F32)
        bias[:, pl.ds(pl.multiple_of(j * 128, 128), 128)] = jnp.where(
            (place >= span_first) & (place < span_after), 0.0, EXCLUDED
        )

    loads[0].wait()
    loads[1].wait()
    lane = lax.broadcasted_iota(jnp.int32, (GLOB, 128), 1)
    stat = jnp.zeros((GLOB, 128), F32)
    for h in range(HERE):
        cols = slice(h * HD, (h + 1) * HD)
        queries = scaled_parts(gq_ref[:, cols])
        scores = dot_nt(queries, twice(kbuf[own, cols])) + bias[...]
        peak = jnp.max(scores, axis=1, keepdims=True)
        weights = jnp.exp2(scores - peak).astype(BF16)
        acc = dot_nn(weights, with_ones(vbuf[own, cols]))
        msg[h] = (acc[:, :HD] / acc[:, HD:]).astype(BF16)
        stat = put_log(stat, h, peak + jnp.log2(acc[:, HD:]), lane)
        if h % 2:
            for d in (2, 1, 3):
                x_copy(d, h - 1).start()
                x_copy(d, h).start()
    msg[HERE] = stat.astype(BF16)
    for d in (2, 1, 3):
        x_copy(d, HERE).start()
    loads[2].wait()

    def after_x():
        for d in range(1, NX):
            for h in range(PARTS):
                x_copy(d, h).wait_recv()
        parts = [[msg[h, x_rows(x), :] for h in range(PARTS)]]
        parts += [[msg_x[d, h] for h in range(PARTS)] for d in range(NX - 1)]
        outs, logs = combine(parts, XB)
        lane = lax.broadcasted_iota(jnp.int32, (XB, 128), 1)
        stat = jnp.zeros((XB, 128), F32)
        for h in range(HERE):
            msg2[h] = outs[h].astype(BF16)
            stat = put_log(stat, h, logs[h], lane)
        msg2[HERE] = stat.astype(BF16)
        for d in range(1, NY):
            y_copy(d).start()

    def after_y():
        for d in range(1, NY):
            y_copy(d).wait_recv()
        parts = [[msg2[h, y_rows(y), :] for h in range(PARTS)]]
        parts += [[msg_y[d, h] for h in range(PARTS)] for d in range(NY - 1)]
        outs, _ = combine(parts, YB)
        gall[head] = jnp.concatenate([o.astype(BF16) for o in outs], axis=1)
        for d in range(1, NHEAD):
            z_copy(d).start()
        halos[2].start()
        halos[3].start()

    def after_z():
        for d in range(1, NHEAD):
            z_copy(d).wait_recv()
        squares = jnp.zeros((YB, 1), F32)
        for g in range(NHEAD):
            wide = gall[g].astype(F32)
            squares = squares + jnp.sum(wide * wide, axis=1, keepdims=True)
        inverse = lax.rsqrt(squares / (NHEAD * WIDTH) + 1e-06)
        loads[3].wait()
        total = jnp.zeros((YB, WIDTH), F32)
        for g in range(NHEAD):
            normed = (gall[g].astype(F32) * inverse).astype(BF16)
            total = total + dot_nn(normed, proj[g * WIDTH:(g + 1) * WIDTH, :])
        gv[mine, :] = total.astype(BF16)
        for d in range(1, NY):
            gy_copy(d).start()

    def after_gy():
        for d in range(1, NY):
            gy_copy(d).wait_recv()
        for d in range(1, NX):
            gx_copy(d).start()

    def place_bias(t, start, width):
        here = pl.ds(pl.multiple_of(t * TILE, TILE), TILE)
        base = (seq * TOK - RADIUS + start).astype(F32)
        shift = (t * TILE - start).astype(F32)
        row = lax.broadcasted_iota(jnp.int32, (TILE, 128), 0).astype(F32) + shift
        lane = lax.broadcasted_iota(jnp.int32, (TILE, 128), 1).astype(F32)
        first = jnp.maximum(as_column(doc_ref[0:1, here], TILE) - base, row)
        after = jnp.minimum(
            as_column(doc_ref[1:2, here], TILE) - base, row + (2 * RADIUS + 1)
        )
        for j in range(width // 128):
            place = lane + float(j * 128)
            local_bias[:, j * 128:(j + 1) * 128] = jnp.where(
                (place >= first) & (place < after), 0.0, EXCLUDED
            )

    def own_keys(t, start, width, slot):
        place_bias(t, start, width)
        here = pl.ds(pl.multiple_of(t * TILE, TILE), TILE)
        window = pl.ds(pl.multiple_of(start, TILE), width)
        for h in range(HERE):
            cols = slice(h * HD, (h + 1) * HD)
            queries = scaled_parts(qbuf[here, cols])
            near = dot_nt(queries, twice(kbuf[window, cols])) + local_bias[:, :width]
            edge = dot_nt(queries, twice(gk_ref[:, cols]))
            peak = jnp.maximum(
                jnp.max(near, axis=1, keepdims=True), jnp.max(edge, axis=1, keepdims=True)
            )
            edges[t, h] = jnp.exp2(edge - peak).astype(BF16)
            near_exp = jnp.exp2(near - peak).astype(BF16)
            sums[t, h] = dot_nn(near_exp, with_ones(vbuf[window, cols]))
            if slot is not None:
                factor[slot, h] = jnp.broadcast_to(peak, (TILE, HD))

    def halo_keys(t, start, width, slot):
        place_bias(t, start, width)
        here = pl.ds(pl.multiple_of(t * TILE, TILE), TILE)
        window = pl.ds(pl.multiple_of(start, TILE), width)
        for h in range(HERE):
            cols = slice(h * HD, (h + 1) * HD)
            queries = scaled_parts(qbuf[here, cols])
            near = dot_nt(queries, twice(kbuf[window, cols])) + local_bias[:, :width]
            peak = jnp.max(near, axis=1, keepdims=True)
            near_exp = jnp.exp2(near - peak).astype(BF16)
            more = dot_nn(near_exp, with_ones(vbuf[window, cols]))
            old = factor[slot, h]
            top = jnp.maximum(old, peak)
            down, added = jnp.exp2(old - top), jnp.exp2(peak - top)
            for c in (slice(0, HD), slice(HD, 2 * HD)):
                sums[t, h, :, c] = sums[t, h, :, c] * down + more[:, c] * added
            factor[slot, h] = down

    first_in = RADIUS // TILE
    last_in = TILES - first_in

    @pl.loop(first_in, last_in)
    def _(t):
        own_keys(t, t * TILE, SPAN, None)
        pl.when(t == first_in)(after_x)
        pl.when(t == first_in + 2)(after_y)

    far, mid = RADIUS + TILE, RADIUS + 2 * TILE

    @pl.loop(0, 2)
    def _(i):
        t = 1 + i * (TILES - 3)
        own_keys(t, RADIUS + i * (TOK - mid), mid, i)
        pl.when(i == 0)(after_z)
        pl.when(i == 1)(after_gy)

    @pl.loop(0, 2)
    def _(i):
        own_keys(i * (TILES - 1), RADIUS + i * (TOK - far), far, 2 + i)

    for c in halos:
        c.wait_recv()

    @pl.loop(0, 2)
    def _(i):
        halo_keys(1 + i * (TILES - 3), TILE + i * (TOK + TILE), TILE, i)
        halo_keys(i * (TILES - 1), i * (TOK + RADIUS), RADIUS, 2 + i)

    for d in range(1, NX):
        gx_copy(d).wait_recv()

    def out_copy(t):
        here = pl.ds(pl.multiple_of(t * TILE, TILE), TILE)
        return pltpu.make_async_copy(obuf.at[here], out_hbm.at[here], out_sems.at[t])

    def finish(t, slot):
        here = pl.ds(pl.multiple_of(t * TILE, TILE), TILE)
        for h in range(HERE):
            cols = slice(h * HD, (h + 1) * HD)
            edge = dot_nn(edges[t, h], with_ones(gv[:, cols]))
            upper, lower = edge[:, :HD], edge[:, HD:]
            if slot is not None:
                upper, lower = upper * factor[slot, h], lower * factor[slot, h]
            upper, lower = upper + sums[t, h, :, :HD], lower + sums[t, h, :, HD:]
            obuf[here, cols] = (upper / lower).astype(BF16)
        out_copy(t).start()

    @pl.loop(first_in, last_in)
    def _(t):
        finish(t, None)

    @pl.loop(0, 2)
    def _(i):
        finish(1 + i * (TILES - 3), i)
        finish(i * (TILES - 1), 2 + i)

    for t in range(TILES):
        out_copy(t).wait()
    for d in range(1, NX):
        for h in range(PARTS):
            x_copy(d, h).wait_send()
        gx_copy(d).wait_send()
    for d in range(1, NY):
        y_copy(d).wait_send()
        gy_copy(d).wait_send()
    for d in range(1, NHEAD):
        z_copy(d).wait_send()
    for c in halos:
        c.wait_send()


def local(queries, keys, values, doc_bounds, global_queries, global_keys, global_span, global_proj):
    anyspec = pl.BlockSpec(memory_space=pl.ANY)
    vmem = pl.BlockSpec(memory_space=pltpu.VMEM)
    dma = pltpu.SemaphoreType.DMA
    return pl.pallas_call(
        kernel,
        out_shape=jax.ShapeDtypeStruct((TOK, WIDTH), BF16),
        in_specs=[vmem] * 4 + [anyspec] * 4,
        out_specs=anyspec,
        scratch_shapes=[
            pltpu.VMEM((TOK, WIDTH), BF16),
            pltpu.VMEM((TOK + 2 * RADIUS, WIDTH), BF16),
            pltpu.VMEM((TOK + 2 * RADIUS, WIDTH), BF16),
            pltpu.VMEM((NHEAD * WIDTH, WIDTH), BF16),
            pltpu.VMEM((GLOB, TOK), F32),
            pltpu.VMEM((TILE, SPAN), F32),
            pltpu.VMEM((TILES, HERE, TILE, 2 * HD), F32),
            pltpu.VMEM((TILES, HERE, TILE, GLOB), BF16),
            pltpu.VMEM((2 * RADIUS // TILE, HERE, TILE, HD), F32),
            pltpu.VMEM((TOK, WIDTH), BF16),
            pltpu.VMEM((PARTS, GLOB, HD), BF16),
            pltpu.VMEM((NX - 1, PARTS, XB, HD), BF16),
            pltpu.VMEM((PARTS, XB, HD), BF16),
            pltpu.VMEM((NY - 1, PARTS, YB, HD), BF16),
            pltpu.VMEM((NHEAD, YB, WIDTH), BF16),
            pltpu.VMEM((GLOB, WIDTH), BF16),
            dma((4,)), dma((TILES,)), dma((4,)), dma((4,)),
            dma((NX - 1, PARTS)), dma((NX - 1, PARTS)), dma((NY - 1,)), dma((NY - 1,)),
            dma((NHEAD - 1,)), dma((NHEAD - 1,)),
            dma((NY - 1,)), dma((NY - 1,)), dma((NX - 1,)), dma((NX - 1,)),
        ],
        compiler_params=pltpu.CompilerParams(
            collective_id=0, has_side_effects=True, vmem_limit_bytes=63 * 2**20
        ),
        name="attention",
    )(
        global_queries, global_keys, global_span, doc_bounds,
        queries, keys, values, global_proj,
    )


def solution(mesh):
    in_specs = (
        P("seq", "head"),
        P("seq", "head"),
        P("seq", "head"),
        P(None, "seq"),
        P(None, "head"),
        P(None, "head"),
        P(),
        P(None, "head"),
    )
    out_specs = P("seq", "head")
    return jax.shard_map(local, mesh=mesh, in_specs=in_specs, out_specs=out_specs, check_vma=False)
```

```python
import functools
import math

import jax
import jax.numpy as jnp
from jax import lax
from jax.experimental import pallas as pl
from jax.experimental.pallas import tpu as pltpu
from jax.sharding import PartitionSpec as P

HD = 128
RADIUS = 512
HERE = 4
TOK = 2048
GLOB = 512
WIDTH = HERE * HD
TILE = 256
SPAN = TILE + 2 * RADIUS
EXCLUDED = -1e30
LOG2_SCALE = math.log2(math.e) / math.sqrt(HD)
NX = 4
NY = 4
NHEAD = 8
XB = GLOB // NX
YB = XB // NY
PARTS = HERE + 1
SIDE = WIDTH // 2
MESH = pl.DeviceIdType.MESH
F32 = jnp.float32
BF16 = jnp.bfloat16


def dot_nt(a, b):
    return lax.dot_general(a, b, (((1,), (1,)), ((), ())), preferred_element_type=F32)


def dot_nn(a, b):
    return jnp.dot(a, b, preferred_element_type=F32)


def twice(k):
    return jnp.concatenate([k, k], axis=1)


def with_ones(v):
    return jnp.concatenate([v, jnp.ones_like(v)], axis=1)


def scaled_parts(q):
    scaled = q.astype(F32) * LOG2_SCALE
    high = scaled.astype(BF16)
    low = (scaled - high.astype(F32)).astype(BF16)
    return jnp.concatenate([high, low], axis=1)


def as_column(row, count):
    return jnp.transpose(jnp.broadcast_to(row.astype(F32), (128, count)))


def combine(parts, rows):
    lane = lax.broadcasted_iota(jnp.int32, (rows, 128), 1)
    stats = [p[HERE].astype(F32) for p in parts]
    outs, logs = [], []
    for h in range(HERE):
        mine = (lane >= 3 * h) & (lane < 3 * h + 3)
        lse = [jnp.sum(jnp.where(mine, s, 0.0), axis=1, keepdims=True) for s in stats]
        top = functools.reduce(jnp.maximum, lse)
        weights = [jnp.exp2(x - top) for x in lse]
        total = functools.reduce(jnp.add, weights)
        acc = functools.reduce(
            jnp.add, [w * p[h].astype(F32) for w, p in zip(weights, parts)]
        )
        outs.append(acc / total)
        logs.append(top + jnp.log2(total))
    return outs, logs


def put_log(stat, h, log, lane):
    high = log.astype(BF16).astype(F32)
    mid = (log - high).astype(BF16).astype(F32)
    low = log - high - mid
    stat = jnp.where(lane == 3 * h, high, stat)
    stat = jnp.where(lane == 3 * h + 1, mid, stat)
    return jnp.where(lane == 3 * h + 2, low, stat)


TILES = TOK // TILE


def kernel(
    gq_ref, gk_ref, span_ref, doc_ref, q_hbm, k_hbm, v_hbm, proj_hbm, out_hbm,
    qbuf, kbuf, vbuf, proj, bias, local_bias, sums, edges, factor, obuf, scores, weights,
    msg, msg_x, msg2, msg_y, gall, gv, gk_turned,
    load_sems, out_sems, halo_send, halo_recv, x_send, x_recv, y_send, y_recv,
    z_send, z_recv, gy_send, gy_recv, gx_send, gx_recv,
):
    seq = lax.axis_index("seq")
    head = lax.axis_index("head")
    x, y = seq // NY, seq % NY
    right = ((seq + 1) % (NX * NY), head)
    left = ((seq + NX * NY - 1) % (NX * NY), head)
    x_peers = [(((x + d) % NX) * NY + y, head) for d in range(1, NX)]
    y_peers = [(x * NY + (y + d) % NY, head) for d in range(1, NY)]
    z_peers = [(seq, (head + d) % NHEAD) for d in range(1, NHEAD)]
    everyone = [left, right] + x_peers + y_peers + z_peers

    def remote(src, dst, send, recv, peer):
        return pltpu.make_async_remote_copy(
            src_ref=src, dst_ref=dst, send_sem=send, recv_sem=recv,
            device_id=peer, device_id_type=MESH,
        )

    def x_rows(b):
        return pl.ds(pl.multiple_of(b * XB, XB), XB)

    def y_rows(b):
        return pl.ds(pl.multiple_of(b * YB, YB), YB)

    own = pl.ds(RADIUS, TOK)
    loads = [
        pltpu.make_async_copy(k_hbm, kbuf.at[own], load_sems.at[0]),
        pltpu.make_async_copy(v_hbm, vbuf.at[own], load_sems.at[1]),
        pltpu.make_async_copy(q_hbm, qbuf, load_sems.at[2]),
        pltpu.make_async_copy(proj_hbm, proj, load_sems.at[3]),
    ]
    front, back = pl.ds(0, RADIUS), pl.ds(TOK - RADIUS, RADIUS)
    before, behind = pl.ds(0, RADIUS), pl.ds(TOK + RADIUS, RADIUS)
    halos = [
        remote(k_hbm.at[back], kbuf.at[before], halo_send.at[0], halo_recv.at[0], right),
        remote(k_hbm.at[front], kbuf.at[behind], halo_send.at[1], halo_recv.at[1], left),
        remote(v_hbm.at[back], vbuf.at[before], halo_send.at[2], halo_recv.at[2], right),
        remote(v_hbm.at[front], vbuf.at[behind], halo_send.at[3], halo_recv.at[3], left),
    ]

    def x_copy(d):
        return remote(
            msg.at[:, x_rows((x + d) % NX)], msg_x.at[d - 1],
            x_send.at[d - 1], x_recv.at[d - 1], x_peers[d - 1],
        )

    def y_copy(d):
        return remote(
            msg2.at[:, y_rows((y + d) % NY)], msg_y.at[d - 1],
            y_send.at[d - 1], y_recv.at[d - 1], y_peers[d - 1],
        )

    def z_copy(d):
        return remote(
            gall.at[head], gall.at[head],
            z_send.at[d - 1], z_recv.at[d - 1], z_peers[d - 1],
        )

    mine = [
        pl.ds(pl.multiple_of(x * XB + y * YB, YB), YB),
        pl.ds(pl.multiple_of(y * XB + x * YB, YB), YB),
    ]

    def first_copy(half, d):
        return remote(
            gv.at[half, mine[half]], gv.at[half, mine[half]],
            gy_send.at[half, d - 1], gy_recv.at[half, d - 1],
            (y_peers, x_peers)[half][d - 1],
        )

    def second_copy(half, d):
        rows = x_rows((x, y)[half])
        return remote(
            gv.at[half, rows], gv.at[half, rows],
            gx_send.at[half, d - 1], gx_recv.at[half, d - 1],
            (x_peers, y_peers)[half][d - 1],
        )

    for c in loads:
        c.start()
    barrier = pltpu.get_barrier_semaphore()
    for peer in everyone:
        pl.semaphore_signal(barrier, inc=1, device_id=peer, device_id_type=MESH)
    for i in range(NX):
        for j in range(NY):
            gk_turned[j * XB + i * YB:j * XB + (i + 1) * YB, :] = gk_ref[
                i * XB + j * YB:i * XB + (j + 1) * YB, SIDE:
            ]
    pl.semaphore_wait(barrier, len(everyone))
    halos[0].start()
    halos[1].start()

    offset = (seq * TOK).astype(F32)
    span_first = as_column(span_ref[0:1, :], GLOB) - offset
    span_after = as_column(span_ref[1:2, :], GLOB) - offset
    lane_f = lax.broadcasted_iota(jnp.int32, (GLOB, 128), 1).astype(F32)

    @pl.loop(0, TOK // 128)
    def _(j):
        place = lane_f + (j * 128).astype(F32)
        bias[:, pl.ds(pl.multiple_of(j * 128, 128), 128)] = jnp.where(
            (place >= span_first) & (place < span_after), 0.0, EXCLUDED
        )

    loads[0].wait()
    loads[1].wait()
    lane = lax.broadcasted_iota(jnp.int32, (GLOB, 128), 1)
    stat = jnp.zeros((GLOB, 128), F32)
    for h in range(HERE):
        cols = slice(h * HD, (h + 1) * HD)
        queries = scaled_parts(gq_ref[:, cols])
        score, weight = scores.at[h % 2], weights.at[h % 2]
        tops = []
        for c in range(0, TOK, TILE):
            part = dot_nt(queries, twice(kbuf[RADIUS + c:RADIUS + c + TILE, cols]))
            part = part + bias[:, c:c + TILE]
            score[:, c:c + TILE] = part
            tops.append(jnp.maximum(part[:, :128], part[:, 128:]))
        peak = jnp.max(functools.reduce(jnp.maximum, tops), axis=1, keepdims=True)
        for c in range(0, TOK, TILE):
            weight[:, c:c + TILE] = jnp.exp2(score[:, c:c + TILE] - peak).astype(BF16)
        acc = dot_nn(weight[...], with_ones(vbuf[own, cols]))
        msg[h] = (acc[:, :HD] / acc[:, HD:]).astype(BF16)
        stat = put_log(stat, h, peak + jnp.log2(acc[:, HD:]), lane)
    msg[HERE] = stat.astype(BF16)
    for d in (2, 1, 3):
        x_copy(d).start()
    loads[2].wait()

    def after_x():
        for d in range(1, NX):
            x_copy(d).wait_recv()
        parts = [[msg[h, x_rows(x), :] for h in range(PARTS)]]
        parts += [[msg_x[d, h] for h in range(PARTS)] for d in range(NX - 1)]
        outs, logs = combine(parts, XB)
        lane = lax.broadcasted_iota(jnp.int32, (XB, 128), 1)
        stat = jnp.zeros((XB, 128), F32)
        for h in range(HERE):
            msg2[h] = outs[h].astype(BF16)
            stat = put_log(stat, h, logs[h], lane)
        msg2[HERE] = stat.astype(BF16)
        for d in range(1, NY):
            y_copy(d).start()

    def after_y():
        for d in range(1, NY):
            y_copy(d).wait_recv()
        parts = [[msg2[h, y_rows(y), :] for h in range(PARTS)]]
        parts += [[msg_y[d, h] for h in range(PARTS)] for d in range(NY - 1)]
        outs, _ = combine(parts, YB)
        gall[head] = jnp.concatenate([o.astype(BF16) for o in outs], axis=1)
        for d in range(1, NHEAD):
            z_copy(d).start()
        halos[2].start()
        halos[3].start()

    def after_z():
        for d in range(1, NHEAD):
            z_copy(d).wait_recv()
        squares = jnp.zeros((YB, 1), F32)
        for g in range(NHEAD):
            wide = gall[g].astype(F32)
            squares = squares + jnp.sum(wide * wide, axis=1, keepdims=True)
        inverse = lax.rsqrt(squares / (NHEAD * WIDTH) + 1e-06)
        loads[3].wait()
        total = jnp.zeros((YB, WIDTH), F32)
        for g in range(NHEAD):
            normed = (gall[g].astype(F32) * inverse).astype(BF16)
            total = total + dot_nn(normed, proj[g * WIDTH:(g + 1) * WIDTH, :])
        for half in range(2):
            gv[half, mine[half], :] = total[:, half * SIDE:(half + 1) * SIDE].astype(BF16)
        for d in range(1, NY):
            for half in range(2):
                first_copy(half, d).start()

    def after_gy():
        for half in range(2):
            for d in range(1, NX):
                first_copy(half, d).wait_recv()
            for d in range(1, NX):
                second_copy(half, d).start()

    def place_bias(t, start, width):
        here = pl.ds(pl.multiple_of(t * TILE, TILE), TILE)
        base = (seq * TOK - RADIUS + start).astype(F32)
        shift = (t * TILE - start).astype(F32)
        row = lax.broadcasted_iota(jnp.int32, (TILE, 128), 0).astype(F32) + shift
        lane = lax.broadcasted_iota(jnp.int32, (TILE, 128), 1).astype(F32)
        first = jnp.maximum(as_column(doc_ref[0:1, here], TILE) - base, row)
        after = jnp.minimum(
            as_column(doc_ref[1:2, here], TILE) - base, row + (2 * RADIUS + 1)
        )
        for j in range(width // 128):
            place = lane + float(j * 128)
            local_bias[:, j * 128:(j + 1) * 128] = jnp.where(
                (place >= first) & (place < after), 0.0, EXCLUDED
            )

    def own_keys(t, start, width, slot):
        place_bias(t, start, width)
        here = pl.ds(pl.multiple_of(t * TILE, TILE), TILE)
        window = pl.ds(pl.multiple_of(start, TILE), width)
        for h in range(HERE):
            cols = slice(h * HD, (h + 1) * HD)
            queries = scaled_parts(qbuf[here, cols])
            score, weight = scores.at[h % 2, :TILE], weights.at[h % 2, :TILE]
            tops = []
            for c in range(0, width, TILE):
                rows = pl.ds(pl.multiple_of(start + c, TILE), TILE)
                part = dot_nt(queries, twice(kbuf[rows, cols])) + local_bias[:, c:c + TILE]
                score[:, c:c + TILE] = part
                tops.append(jnp.maximum(part[:, :128], part[:, 128:]))
            edge_keys = gk_ref[:, cols] if h < 2 else gk_turned[:, (h - 2) * HD:(h - 1) * HD]
            for c in range(0, GLOB, TILE):
                part = dot_nt(queries, twice(edge_keys[c:c + TILE]))
                score[:, width + c:width + c + TILE] = part
                tops.append(jnp.maximum(part[:, :128], part[:, 128:]))
            peak = jnp.max(functools.reduce(jnp.maximum, tops), axis=1, keepdims=True)
            for c in range(0, width, TILE):
                weight[:, c:c + TILE] = jnp.exp2(score[:, c:c + TILE] - peak).astype(BF16)
            for c in range(0, GLOB, TILE):
                edges[t, h, :, c:c + TILE] = jnp.exp2(
                    score[:, width + c:width + c + TILE] - peak
                ).astype(BF16)
            sums[t, h] = dot_nn(weight[:, :width], with_ones(vbuf[window, cols]))
            if slot is not None:
                factor[slot, h] = jnp.broadcast_to(peak, (TILE, HD))

    def halo_keys(t, start, width, slot):
        place_bias(t, start, width)
        here = pl.ds(pl.multiple_of(t * TILE, TILE), TILE)
        window = pl.ds(pl.multiple_of(start, TILE), width)
        for h in range(HERE):
            cols = slice(h * HD, (h + 1) * HD)
            queries = scaled_parts(qbuf[here, cols])
            near = dot_nt(queries, twice(kbuf[window, cols])) + local_bias[:, :width]
            peak = jnp.max(near, axis=1, keepdims=True)
            near_exp = jnp.exp2(near - peak).astype(BF16)
            more = dot_nn(near_exp, with_ones(vbuf[window, cols]))
            old = factor[slot, h]
            top = jnp.maximum(old, peak)
            down, added = jnp.exp2(old - top), jnp.exp2(peak - top)
            for c in (slice(0, HD), slice(HD, 2 * HD)):
                sums[t, h, :, c] = sums[t, h, :, c] * down + more[:, c] * added
            factor[slot, h] = down

    first_in = RADIUS // TILE
    last_in = TILES - first_in

    @pl.loop(first_in, last_in)
    def _(t):
        own_keys(t, t * TILE, SPAN, None)
        pl.when(t == first_in)(after_x)
        pl.when(t == first_in + 2)(after_y)

    far, mid = RADIUS + TILE, RADIUS + 2 * TILE

    @pl.loop(0, 2)
    def _(i):
        t = 1 + i * (TILES - 3)
        own_keys(t, RADIUS + i * (TOK - mid), mid, i)
        pl.when(i == 0)(after_z)
        pl.when(i == 1)(after_gy)

    @pl.loop(0, 2)
    def _(i):
        own_keys(i * (TILES - 1), RADIUS + i * (TOK - far), far, 2 + i)

    for c in halos:
        c.wait_recv()

    @pl.loop(0, 2)
    def _(i):
        halo_keys(1 + i * (TILES - 3), TILE + i * (TOK + TILE), TILE, i)
        halo_keys(i * (TILES - 1), i * (TOK + RADIUS), RADIUS, 2 + i)

    for half in range(2):
        for d in range(1, NX):
            second_copy(half, d).wait_recv()

    def out_copy(t):
        here = pl.ds(pl.multiple_of(t * TILE, TILE), TILE)
        return pltpu.make_async_copy(obuf.at[here], out_hbm.at[here], out_sems.at[t])

    def finish(t, slot):
        here = pl.ds(pl.multiple_of(t * TILE, TILE), TILE)
        for h in range(HERE):
            cols = slice(h * HD, (h + 1) * HD)
            edge = dot_nn(edges[t, h], with_ones(gv[h // 2, :, (h % 2) * HD:(h % 2 + 1) * HD]))
            upper, lower = edge[:, :HD], edge[:, HD:]
            if slot is not None:
                upper, lower = upper * factor[slot, h], lower * factor[slot, h]
            upper, lower = upper + sums[t, h, :, :HD], lower + sums[t, h, :, HD:]
            obuf[here, cols] = (upper / lower).astype(BF16)
        out_copy(t).start()

    @pl.loop(first_in, last_in)
    def _(t):
        finish(t, None)

    @pl.loop(0, 2)
    def _(i):
        finish(1 + i * (TILES - 3), i)
        finish(i * (TILES - 1), 2 + i)

    for t in range(TILES):
        out_copy(t).wait()
    for d in range(1, NX):
        x_copy(d).wait_send()
        y_copy(d).wait_send()
        for half in range(2):
            first_copy(half, d).wait_send()
            second_copy(half, d).wait_send()
    for d in range(1, NHEAD):
        z_copy(d).wait_send()
    for c in halos:
        c.wait_send()


def local(queries, keys, values, doc_bounds, global_queries, global_keys, global_span, global_proj):
    anyspec = pl.BlockSpec(memory_space=pl.ANY)
    vmem = pl.BlockSpec(memory_space=pltpu.VMEM)
    dma = pltpu.SemaphoreType.DMA
    return pl.pallas_call(
        kernel,
        out_shape=jax.ShapeDtypeStruct((TOK, WIDTH), BF16),
        in_specs=[vmem] * 4 + [anyspec] * 4,
        out_specs=anyspec,
        scratch_shapes=[
            pltpu.VMEM((TOK, WIDTH), BF16),
            pltpu.VMEM((TOK + 2 * RADIUS, WIDTH), BF16),
            pltpu.VMEM((TOK + 2 * RADIUS, WIDTH), BF16),
            pltpu.VMEM((NHEAD * WIDTH, WIDTH), BF16),
            pltpu.VMEM((GLOB, TOK), F32),
            pltpu.VMEM((TILE, SPAN), F32),
            pltpu.VMEM((TILES, HERE, TILE, 2 * HD), F32),
            pltpu.VMEM((TILES, HERE, TILE, GLOB), BF16),
            pltpu.VMEM((2 * RADIUS // TILE, HERE, TILE, HD), F32),
            pltpu.VMEM((TOK, WIDTH), BF16),
            pltpu.VMEM((2, GLOB, TOK), F32),
            pltpu.VMEM((2, GLOB, TOK), BF16),
            pltpu.VMEM((PARTS, GLOB, HD), BF16),
            pltpu.VMEM((NX - 1, PARTS, XB, HD), BF16),
            pltpu.VMEM((PARTS, XB, HD), BF16),
            pltpu.VMEM((NY - 1, PARTS, YB, HD), BF16),
            pltpu.VMEM((NHEAD, YB, WIDTH), BF16),
            pltpu.VMEM((2, GLOB, SIDE), BF16),
            pltpu.VMEM((GLOB, SIDE), BF16),
            dma((4,)), dma((TILES,)), dma((4,)), dma((4,)),
            dma((NX - 1,)), dma((NX - 1,)), dma((NY - 1,)), dma((NY - 1,)),
            dma((NHEAD - 1,)), dma((NHEAD - 1,)),
            dma((2, NY - 1)), dma((2, NY - 1)), dma((2, NX - 1)), dma((2, NX - 1)),
        ],
        compiler_params=pltpu.CompilerParams(
            collective_id=0, has_side_effects=True, vmem_limit_bytes=63 * 2**20
        ),
        name="attention",
    )(
        global_queries, global_keys, global_span, doc_bounds,
        queries, keys, values, global_proj,
    )


def solution(mesh):
    in_specs = (
        P("seq", "head"),
        P("seq", "head"),
        P("seq", "head"),
        P(None, "seq"),
        P(None, "head"),
        P(None, "head"),
        P(),
        P(None, "head"),
    )
    out_specs = P("seq", "head")
    return jax.shard_map(local, mesh=mesh, in_specs=in_specs, out_specs=out_specs, check_vma=False)
```

```python
import functools
import math

import jax
import jax.numpy as jnp
from jax import lax
from jax.experimental import pallas as pl
from jax.experimental.pallas import tpu as pltpu
from jax.sharding import PartitionSpec as P

HD = 128
RADIUS = 512
HERE = 4
TOK = 2048
GLOB = 512
WIDTH = HERE * HD
TILE = 256
SPAN = TILE + 2 * RADIUS
EXCLUDED = -1e30
LOG2_SCALE = math.log2(math.e) / math.sqrt(HD)
NX = 4
NY = 4
NHEAD = 8
XB = GLOB // NX
YB = XB // NY
PAIR = HERE // 2
PIECES = 4
PIECE = RADIUS // PIECES
HALO_PLAN = (2, 0, 4, 1, 1)
PARTS = PAIR + 1
SIDE = WIDTH // 2
MESH = pl.DeviceIdType.MESH
F32 = jnp.float32
BF16 = jnp.bfloat16


def dot_nt(a, b):
    return lax.dot_general(a, b, (((1,), (1,)), ((), ())), preferred_element_type=F32)


def dot_nn(a, b):
    return jnp.dot(a, b, preferred_element_type=F32)


def twice(k):
    return jnp.concatenate([k, k], axis=1)


def with_ones(v):
    return jnp.concatenate([v, jnp.ones_like(v)], axis=1)


def scaled_parts(q):
    scaled = q.astype(F32) * LOG2_SCALE
    high = scaled.astype(BF16)
    low = (scaled - high.astype(F32)).astype(BF16)
    return jnp.concatenate([high, low], axis=1)


def as_column(row, count):
    return jnp.transpose(jnp.broadcast_to(row.astype(F32), (128, count)))


def combine(parts, rows):
    lane = lax.broadcasted_iota(jnp.int32, (rows, 128), 1)
    stats = [p[PAIR].astype(F32) for p in parts]
    outs, logs = [], []
    for h in range(PAIR):
        mine = (lane >= 3 * h) & (lane < 3 * h + 3)
        lse = [jnp.sum(jnp.where(mine, s, 0.0), axis=1, keepdims=True) for s in stats]
        top = functools.reduce(jnp.maximum, lse)
        weights = [jnp.exp2(x - top) for x in lse]
        total = functools.reduce(jnp.add, weights)
        acc = functools.reduce(
            jnp.add, [w * p[h].astype(F32) for w, p in zip(weights, parts)]
        )
        outs.append(acc / total)
        logs.append(top + jnp.log2(total))
    return outs, logs


def put_log(stat, h, log, lane):
    high = log.astype(BF16).astype(F32)
    mid = (log - high).astype(BF16).astype(F32)
    low = log - high - mid
    stat = jnp.where(lane == 3 * h, high, stat)
    stat = jnp.where(lane == 3 * h + 1, mid, stat)
    return jnp.where(lane == 3 * h + 2, low, stat)


TILES = TOK // TILE


def kernel(
    gq_ref, gk_ref, span_ref, doc_ref, q_hbm, k_hbm, v_hbm, proj_hbm, out_hbm,
    qbuf, kbuf, vbuf, proj, bias, local_bias, sums, edges, factor, obuf, scores, weights,
    msg, msg_x, msg2, msg_y, gall, gv, gk_turned,
    load_sems, out_sems, halo_send, halo_recv, x_send, x_recv, y_send, y_recv,
    z_send, z_recv, gy_send, gy_recv, gx_send, gx_recv,
):
    seq = lax.axis_index("seq")
    head = lax.axis_index("head")
    x, y = seq // NY, seq % NY
    right = ((seq + 1) % (NX * NY), head)
    left = ((seq + NX * NY - 1) % (NX * NY), head)
    x_peers = [(((x + d) % NX) * NY + y, head) for d in range(1, NX)]
    y_peers = [(x * NY + (y + d) % NY, head) for d in range(1, NY)]
    z_peers = [(seq, (head + d) % NHEAD) for d in range(1, NHEAD)]
    everyone = [left, right] + x_peers + y_peers + z_peers

    def remote(src, dst, send, recv, peer):
        return pltpu.make_async_remote_copy(
            src_ref=src, dst_ref=dst, send_sem=send, recv_sem=recv,
            device_id=peer, device_id_type=MESH,
        )

    def x_rows(b):
        return pl.ds(pl.multiple_of(b * XB, XB), XB)

    def y_rows(b):
        return pl.ds(pl.multiple_of(b * YB, YB), YB)

    own = pl.ds(RADIUS, TOK)
    loads = [
        pltpu.make_async_copy(k_hbm, kbuf.at[own], load_sems.at[0]),
        pltpu.make_async_copy(v_hbm, vbuf.at[own], load_sems.at[1]),
        pltpu.make_async_copy(q_hbm, qbuf, load_sems.at[2]),
        pltpu.make_async_copy(proj_hbm, proj, load_sems.at[3]),
    ]
    def halo_pair(c):
        src, dst = (k_hbm, kbuf) if c < PIECES else (v_hbm, vbuf)
        at = (c % PIECES) * PIECE
        return [
            remote(
                src.at[pl.ds(TOK - RADIUS + at, PIECE)], dst.at[pl.ds(at, PIECE)],
                halo_send.at[0, c], halo_recv.at[0, c], right,
            ),
            remote(
                src.at[pl.ds(at, PIECE)], dst.at[pl.ds(TOK + RADIUS + at, PIECE)],
                halo_send.at[1, c], halo_recv.at[1, c], left,
            ),
        ]

    def send_halos(stage):
        first = sum(HALO_PLAN[:stage])
        for c in range(first, first + HALO_PLAN[stage]):
            for copy in halo_pair(c):
                copy.start()

    block = (x, y)
    line_peers = (x_peers, y_peers)

    def part_copy(half, d):
        return remote(
            msg.at[half, :, x_rows((block[half] + d) % NX)], msg_x.at[half, d - 1],
            x_send.at[half, d - 1], x_recv.at[half, d - 1], line_peers[half][d - 1],
        )

    def merge_copy(half, d):
        return remote(
            msg2.at[half, :, y_rows((block[1 - half] + d) % NY)], msg_y.at[half, d - 1],
            y_send.at[half, d - 1], y_recv.at[half, d - 1], line_peers[1 - half][d - 1],
        )

    def z_copy(d):
        return remote(
            gall.at[head], gall.at[head],
            z_send.at[d - 1], z_recv.at[d - 1], z_peers[d - 1],
        )

    mine = [
        pl.ds(pl.multiple_of(x * XB + y * YB, YB), YB),
        pl.ds(pl.multiple_of(y * XB + x * YB, YB), YB),
    ]

    def first_copy(half, d):
        return remote(
            gv.at[half, mine[half]], gv.at[half, mine[half]],
            gy_send.at[half, d - 1], gy_recv.at[half, d - 1],
            (y_peers, x_peers)[half][d - 1],
        )

    def second_copy(half, d):
        rows = x_rows((x, y)[half])
        return remote(
            gv.at[half, rows], gv.at[half, rows],
            gx_send.at[half, d - 1], gx_recv.at[half, d - 1],
            (x_peers, y_peers)[half][d - 1],
        )

    for c in loads:
        c.start()
    barrier = pltpu.get_barrier_semaphore()
    for peer in everyone:
        pl.semaphore_signal(barrier, inc=1, device_id=peer, device_id_type=MESH)
    for i in range(NX):
        for j in range(NY):
            gk_turned[j * XB + i * YB:j * XB + (i + 1) * YB, :] = gk_ref[
                i * XB + j * YB:i * XB + (j + 1) * YB, SIDE:
            ]
    pl.semaphore_wait(barrier, len(everyone))
    send_halos(0)

    offset = (seq * TOK).astype(F32)
    span_first = as_column(span_ref[0:1, :], GLOB) - offset
    span_after = as_column(span_ref[1:2, :], GLOB) - offset
    lane_f = lax.broadcasted_iota(jnp.int32, (GLOB, 128), 1).astype(F32)

    @pl.loop(0, TOK // 128)
    def _(j):
        place = lane_f + (j * 128).astype(F32)
        bias[:, pl.ds(pl.multiple_of(j * 128, 128), 128)] = jnp.where(
            (place >= span_first) & (place < span_after), 0.0, EXCLUDED
        )

    loads[0].wait()
    loads[1].wait()
    lane = lax.broadcasted_iota(jnp.int32, (GLOB, 128), 1)
    stats = [jnp.zeros((GLOB, 128), F32)] * 2

    def put_rows(half, part, rows):
        if half == 0:
            msg[half, part] = rows
            return
        for i in range(NX):
            for j in range(NY):
                msg[half, part, j * XB + i * YB:j * XB + (i + 1) * YB, :] = rows[
                    i * XB + j * YB:i * XB + (j + 1) * YB
                ]

    for h in range(HERE):
        half, part_at = h // PAIR, h % PAIR
        cols = slice(h * HD, (h + 1) * HD)
        queries = scaled_parts(gq_ref[:, cols])
        score, weight = scores.at[h % 2], weights.at[h % 2]
        tops = []
        for c in range(0, TOK, TILE):
            part = dot_nt(queries, twice(kbuf[RADIUS + c:RADIUS + c + TILE, cols]))
            part = part + bias[:, c:c + TILE]
            score[:, c:c + TILE] = part
            tops.append(jnp.maximum(part[:, :128], part[:, 128:]))
        peak = jnp.max(functools.reduce(jnp.maximum, tops), axis=1, keepdims=True)
        for c in range(0, TOK, TILE):
            weight[:, c:c + TILE] = jnp.exp2(score[:, c:c + TILE] - peak).astype(BF16)
        acc = dot_nn(weight[...], with_ones(vbuf[own, cols]))
        put_rows(half, part_at, (acc[:, :HD] / acc[:, HD:]).astype(BF16))
        stats[half] = put_log(stats[half], part_at, peak + jnp.log2(acc[:, HD:]), lane)
    for half in range(2):
        put_rows(half, PAIR, stats[half].astype(BF16))
    for d in (2, 1, 3):
        for half in range(2):
            part_copy(half, d).start()
    loads[2].wait()

    def after_x():
        lane = lax.broadcasted_iota(jnp.int32, (XB, 128), 1)
        for half in range(2):
            for d in range(1, NX):
                part_copy(half, d).wait_recv()
        for half in range(2):
            mine = x_rows(block[half])
            parts = [[msg[half, h, mine, :] for h in range(PARTS)]]
            parts += [[msg_x[half, d, h] for h in range(PARTS)] for d in range(NX - 1)]
            outs, logs = combine(parts, XB)
            stat = jnp.zeros((XB, 128), F32)
            for h in range(PAIR):
                msg2[half, h] = outs[h].astype(BF16)
                stat = put_log(stat, h, logs[h], lane)
            msg2[half, PAIR] = stat.astype(BF16)
        for d in range(1, NY):
            for half in range(2):
                merge_copy(half, d).start()
        send_halos(1)

    def after_y():
        for half in range(2):
            for d in range(1, NY):
                merge_copy(half, d).wait_recv()
        merged = []
        for half in range(2):
            mine = y_rows(block[1 - half])
            parts = [[msg2[half, h, mine, :] for h in range(PARTS)]]
            parts += [[msg_y[half, d, h] for h in range(PARTS)] for d in range(NY - 1)]
            merged += combine(parts, YB)[0]
        gall[head] = jnp.concatenate([o.astype(BF16) for o in merged], axis=1)
        for d in range(1, NHEAD):
            z_copy(d).start()
        send_halos(2)

    def after_z():
        for d in range(1, NHEAD):
            z_copy(d).wait_recv()
        squares = jnp.zeros((YB, 1), F32)
        for g in range(NHEAD):
            wide = gall[g].astype(F32)
            squares = squares + jnp.sum(wide * wide, axis=1, keepdims=True)
        inverse = lax.rsqrt(squares / (NHEAD * WIDTH) + 1e-06)
        loads[3].wait()
        total = jnp.zeros((YB, WIDTH), F32)
        for g in range(NHEAD):
            normed = (gall[g].astype(F32) * inverse).astype(BF16)
            total = total + dot_nn(normed, proj[g * WIDTH:(g + 1) * WIDTH, :])
        for half in range(2):
            gv[half, mine[half], :] = total[:, half * SIDE:(half + 1) * SIDE].astype(BF16)
        for d in range(1, NY):
            for half in range(2):
                first_copy(half, d).start()
        send_halos(3)

    def after_gy():
        for half in range(2):
            for d in range(1, NX):
                first_copy(half, d).wait_recv()
            for d in range(1, NX):
                second_copy(half, d).start()
        send_halos(4)

    def place_bias(t, start, width):
        here = pl.ds(pl.multiple_of(t * TILE, TILE), TILE)
        base = (seq * TOK - RADIUS + start).astype(F32)
        shift = (t * TILE - start).astype(F32)
        row = lax.broadcasted_iota(jnp.int32, (TILE, 128), 0).astype(F32) + shift
        lane = lax.broadcasted_iota(jnp.int32, (TILE, 128), 1).astype(F32)
        first = jnp.maximum(as_column(doc_ref[0:1, here], TILE) - base, row)
        after = jnp.minimum(
            as_column(doc_ref[1:2, here], TILE) - base, row + (2 * RADIUS + 1)
        )
        for j in range(width // 128):
            place = lane + float(j * 128)
            local_bias[:, j * 128:(j + 1) * 128] = jnp.where(
                (place >= first) & (place < after), 0.0, EXCLUDED
            )

    def own_keys(t, start, width, slot):
        place_bias(t, start, width)
        here = pl.ds(pl.multiple_of(t * TILE, TILE), TILE)
        window = pl.ds(pl.multiple_of(start, TILE), width)
        for h in range(HERE):
            cols = slice(h * HD, (h + 1) * HD)
            queries = scaled_parts(qbuf[here, cols])
            score, weight = scores.at[h % 2, :TILE], weights.at[h % 2, :TILE]
            tops = []
            for c in range(0, width, TILE):
                rows = pl.ds(pl.multiple_of(start + c, TILE), TILE)
                part = dot_nt(queries, twice(kbuf[rows, cols])) + local_bias[:, c:c + TILE]
                score[:, c:c + TILE] = part
                tops.append(jnp.maximum(part[:, :128], part[:, 128:]))
            edge_keys = gk_ref[:, cols] if h < 2 else gk_turned[:, (h - 2) * HD:(h - 1) * HD]
            for c in range(0, GLOB, TILE):
                part = dot_nt(queries, twice(edge_keys[c:c + TILE]))
                score[:, width + c:width + c + TILE] = part
                tops.append(jnp.maximum(part[:, :128], part[:, 128:]))
            peak = jnp.max(functools.reduce(jnp.maximum, tops), axis=1, keepdims=True)
            for c in range(0, width, TILE):
                weight[:, c:c + TILE] = jnp.exp2(score[:, c:c + TILE] - peak).astype(BF16)
            for c in range(0, GLOB, TILE):
                edges[t, h, :, c:c + TILE] = jnp.exp2(
                    score[:, width + c:width + c + TILE] - peak
                ).astype(BF16)
            sums[t, h] = dot_nn(weight[:, :width], with_ones(vbuf[window, cols]))
            if slot is not None:
                factor[slot, h] = jnp.broadcast_to(peak, (TILE, HD))

    def halo_keys(t, start, width, slot):
        place_bias(t, start, width)
        here = pl.ds(pl.multiple_of(t * TILE, TILE), TILE)
        window = pl.ds(pl.multiple_of(start, TILE), width)
        for h in range(HERE):
            cols = slice(h * HD, (h + 1) * HD)
            queries = scaled_parts(qbuf[here, cols])
            near = dot_nt(queries, twice(kbuf[window, cols])) + local_bias[:, :width]
            peak = jnp.max(near, axis=1, keepdims=True)
            near_exp = jnp.exp2(near - peak).astype(BF16)
            more = dot_nn(near_exp, with_ones(vbuf[window, cols]))
            old = factor[slot, h]
            top = jnp.maximum(old, peak)
            down, added = jnp.exp2(old - top), jnp.exp2(peak - top)
            for c in (slice(0, HD), slice(HD, 2 * HD)):
                sums[t, h, :, c] = sums[t, h, :, c] * down + more[:, c] * added
            factor[slot, h] = down

    first_in = RADIUS // TILE
    last_in = TILES - first_in

    @pl.loop(first_in, last_in)
    def _(t):
        own_keys(t, t * TILE, SPAN, None)
        pl.when(t == first_in + 1)(after_x)
        pl.when(t == first_in + 2)(after_y)

    far, mid = RADIUS + TILE, RADIUS + 2 * TILE

    @pl.loop(0, 2)
    def _(i):
        t = 1 + i * (TILES - 3)
        own_keys(t, RADIUS + i * (TOK - mid), mid, i)
        pl.when(i == 0)(after_z)
        pl.when(i == 1)(after_gy)

    @pl.loop(0, 2)
    def _(i):
        own_keys(i * (TILES - 1), RADIUS + i * (TOK - far), far, 2 + i)

    for c in range(2 * PIECES):
        for copy in halo_pair(c):
            copy.wait_recv()

    @pl.loop(0, 2)
    def _(i):
        halo_keys(1 + i * (TILES - 3), TILE + i * (TOK + TILE), TILE, i)
        halo_keys(i * (TILES - 1), i * (TOK + RADIUS), RADIUS, 2 + i)

    for half in range(2):
        for d in range(1, NX):
            second_copy(half, d).wait_recv()

    def out_copy(t):
        here = pl.ds(pl.multiple_of(t * TILE, TILE), TILE)
        return pltpu.make_async_copy(obuf.at[here], out_hbm.at[here], out_sems.at[t])

    def finish(t, slot):
        here = pl.ds(pl.multiple_of(t * TILE, TILE), TILE)
        for h in range(HERE):
            cols = slice(h * HD, (h + 1) * HD)
            edge = dot_nn(edges[t, h], with_ones(gv[h // 2, :, (h % 2) * HD:(h % 2 + 1) * HD]))
            upper, lower = edge[:, :HD], edge[:, HD:]
            if slot is not None:
                upper, lower = upper * factor[slot, h], lower * factor[slot, h]
            upper, lower = upper + sums[t, h, :, :HD], lower + sums[t, h, :, HD:]
            obuf[here, cols] = (upper / lower).astype(BF16)
        out_copy(t).start()

    @pl.loop(first_in, last_in)
    def _(t):
        finish(t, None)

    @pl.loop(0, 2)
    def _(i):
        finish(1 + i * (TILES - 3), i)
        finish(i * (TILES - 1), 2 + i)

    for t in range(TILES):
        out_copy(t).wait()
    for d in range(1, NX):
        for half in range(2):
            part_copy(half, d).wait_send()
            merge_copy(half, d).wait_send()
            first_copy(half, d).wait_send()
            second_copy(half, d).wait_send()
    for d in range(1, NHEAD):
        z_copy(d).wait_send()
    for c in range(2 * PIECES):
        for copy in halo_pair(c):
            copy.wait_send()


def local(queries, keys, values, doc_bounds, global_queries, global_keys, global_span, global_proj):
    anyspec = pl.BlockSpec(memory_space=pl.ANY)
    vmem = pl.BlockSpec(memory_space=pltpu.VMEM)
    dma = pltpu.SemaphoreType.DMA
    return pl.pallas_call(
        kernel,
        out_shape=jax.ShapeDtypeStruct((TOK, WIDTH), BF16),
        in_specs=[vmem] * 4 + [anyspec] * 4,
        out_specs=anyspec,
        scratch_shapes=[
            pltpu.VMEM((TOK, WIDTH), BF16),
            pltpu.VMEM((TOK + 2 * RADIUS, WIDTH), BF16),
            pltpu.VMEM((TOK + 2 * RADIUS, WIDTH), BF16),
            pltpu.VMEM((NHEAD * WIDTH, WIDTH), BF16),
            pltpu.VMEM((GLOB, TOK), F32),
            pltpu.VMEM((TILE, SPAN), F32),
            pltpu.VMEM((TILES, HERE, TILE, 2 * HD), F32),
            pltpu.VMEM((TILES, HERE, TILE, GLOB), BF16),
            pltpu.VMEM((2 * RADIUS // TILE, HERE, TILE, HD), F32),
            pltpu.VMEM((TOK, WIDTH), BF16),
            pltpu.VMEM((2, GLOB, TOK), F32),
            pltpu.VMEM((2, GLOB, TOK), BF16),
            pltpu.VMEM((2, PARTS, GLOB, HD), BF16),
            pltpu.VMEM((2, NX - 1, PARTS, XB, HD), BF16),
            pltpu.VMEM((2, PARTS, XB, HD), BF16),
            pltpu.VMEM((2, NY - 1, PARTS, YB, HD), BF16),
            pltpu.VMEM((NHEAD, YB, WIDTH), BF16),
            pltpu.VMEM((2, GLOB, SIDE), BF16),
            pltpu.VMEM((GLOB, SIDE), BF16),
            dma((4,)), dma((TILES,)), dma((2, 2 * PIECES)), dma((2, 2 * PIECES)),
            dma((2, NX - 1)), dma((2, NX - 1)), dma((2, NY - 1)), dma((2, NY - 1)),
            dma((NHEAD - 1,)), dma((NHEAD - 1,)),
            dma((2, NY - 1)), dma((2, NY - 1)), dma((2, NX - 1)), dma((2, NX - 1)),
        ],
        compiler_params=pltpu.CompilerParams(
            collective_id=0, has_side_effects=True, vmem_limit_bytes=63 * 2**20
        ),
        name="attention",
    )(
        global_queries, global_keys, global_span, doc_bounds,
        queries, keys, values, global_proj,
    )


def solution(mesh):
    in_specs = (
        P("seq", "head"),
        P("seq", "head"),
        P("seq", "head"),
        P(None, "seq"),
        P(None, "head"),
        P(None, "head"),
        P(),
        P(None, "head"),
    )
    out_specs = P("seq", "head")
    return jax.shard_map(local, mesh=mesh, in_specs=in_specs, out_specs=out_specs, check_vma=False)
```

```python
import functools
import math

import jax
import jax.numpy as jnp
from jax import lax
from jax.experimental import pallas as pl
from jax.experimental.pallas import tpu as pltpu
from jax.sharding import PartitionSpec as P

HD = 128
RADIUS = 512
HERE = 4
TOK = 2048
GLOB = 512
WIDTH = HERE * HD
TILE = 256
SPAN = TILE + 2 * RADIUS
EXCLUDED = -1e30
LOG2_SCALE = math.log2(math.e) / math.sqrt(HD)
NX = 4
NY = 4
NHEAD = 8
XB = GLOB // NX
YB = XB // NY
PAIR = HERE // 2
PIECES = 4
PIECE = RADIUS // PIECES
HALO_PLAN = (2, 1, 3, 1, 1)
PARTS = PAIR + 1
SIDE = WIDTH // 2
MESH = pl.DeviceIdType.MESH
F32 = jnp.float32
BF16 = jnp.bfloat16


def dot_nt(a, b):
    return lax.dot_general(a, b, (((1,), (1,)), ((), ())), preferred_element_type=F32)


def dot_nn(a, b):
    return jnp.dot(a, b, preferred_element_type=F32)


def twice(k):
    return jnp.concatenate([k, k], axis=1)


def with_ones(v):
    return jnp.concatenate([v, jnp.ones_like(v)], axis=1)


def scaled_parts(q):
    scaled = q.astype(F32) * LOG2_SCALE
    high = scaled.astype(BF16)
    low = (scaled - high.astype(F32)).astype(BF16)
    return jnp.concatenate([high, low], axis=1)


def as_column(row, count):
    return jnp.transpose(jnp.broadcast_to(row.astype(F32), (128, count)))


def combine(parts, rows):
    lane = lax.broadcasted_iota(jnp.int32, (rows, 128), 1)
    stats = [p[PAIR].astype(F32) for p in parts]
    outs, logs = [], []
    for h in range(PAIR):
        mine = (lane >= 3 * h) & (lane < 3 * h + 3)
        lse = [jnp.sum(jnp.where(mine, s, 0.0), axis=1, keepdims=True) for s in stats]
        top = functools.reduce(jnp.maximum, lse)
        weights = [jnp.exp2(x - top) for x in lse]
        total = functools.reduce(jnp.add, weights)
        acc = functools.reduce(
            jnp.add, [w * p[h].astype(F32) for w, p in zip(weights, parts)]
        )
        outs.append(acc / total)
        logs.append(top + jnp.log2(total))
    return outs, logs


def put_log(stat, h, log, lane):
    high = log.astype(BF16).astype(F32)
    mid = (log - high).astype(BF16).astype(F32)
    low = log - high - mid
    stat = jnp.where(lane == 3 * h, high, stat)
    stat = jnp.where(lane == 3 * h + 1, mid, stat)
    return jnp.where(lane == 3 * h + 2, low, stat)


TILES = TOK // TILE


def kernel(
    gq_ref, gk_ref, span_ref, doc_ref, q_hbm, k_hbm, v_hbm, proj_hbm, out_hbm,
    qbuf, kbuf, vbuf, proj, bias, local_bias, sums, edges, factor, obuf, scores, weights,
    msg, msg_x, msg2, msg_y, gall, gv, gk_turned,
    load_sems, out_sems, halo_send, halo_recv, x_send, x_recv, y_send, y_recv,
    z_send, z_recv, gy_send, gy_recv, gx_send, gx_recv,
):
    seq = lax.axis_index("seq")
    head = lax.axis_index("head")
    x, y = seq // NY, seq % NY
    right = ((seq + 1) % (NX * NY), head)
    left = ((seq + NX * NY - 1) % (NX * NY), head)
    x_peers = [(((x + d) % NX) * NY + y, head) for d in range(1, NX)]
    y_peers = [(x * NY + (y + d) % NY, head) for d in range(1, NY)]
    z_peers = [(seq, (head + d) % NHEAD) for d in range(1, NHEAD)]
    everyone = [left, right] + x_peers + y_peers + z_peers

    def remote(src, dst, send, recv, peer):
        return pltpu.make_async_remote_copy(
            src_ref=src, dst_ref=dst, send_sem=send, recv_sem=recv,
            device_id=peer, device_id_type=MESH,
        )

    def x_rows(b):
        return pl.ds(pl.multiple_of(b * XB, XB), XB)

    def y_rows(b):
        return pl.ds(pl.multiple_of(b * YB, YB), YB)

    own = pl.ds(RADIUS, TOK)
    loads = [
        pltpu.make_async_copy(k_hbm, kbuf.at[own], load_sems.at[0]),
        pltpu.make_async_copy(v_hbm, vbuf.at[own], load_sems.at[1]),
        pltpu.make_async_copy(q_hbm, qbuf, load_sems.at[2]),
        pltpu.make_async_copy(proj_hbm, proj, load_sems.at[3]),
    ]
    def halo_pair(c):
        src, dst = (k_hbm, kbuf) if c < PIECES else (v_hbm, vbuf)
        at = (c % PIECES) * PIECE
        return [
            remote(
                src.at[pl.ds(TOK - RADIUS + at, PIECE)], dst.at[pl.ds(at, PIECE)],
                halo_send.at[0, c], halo_recv.at[0, c], right,
            ),
            remote(
                src.at[pl.ds(at, PIECE)], dst.at[pl.ds(TOK + RADIUS + at, PIECE)],
                halo_send.at[1, c], halo_recv.at[1, c], left,
            ),
        ]

    def send_halos(stage):
        first = sum(HALO_PLAN[:stage])
        for c in range(first, first + HALO_PLAN[stage]):
            for copy in halo_pair(c):
                copy.start()

    block = (x, y)
    line_peers = (x_peers, y_peers)

    def part_copy(half, d):
        return remote(
            msg.at[half, :, x_rows((block[half] + d) % NX)], msg_x.at[half, d - 1],
            x_send.at[half, d - 1], x_recv.at[half, d - 1], line_peers[half][d - 1],
        )

    def merge_copy(half, d):
        return remote(
            msg2.at[half, :, y_rows((block[1 - half] + d) % NY)], msg_y.at[half, d - 1],
            y_send.at[half, d - 1], y_recv.at[half, d - 1], line_peers[1 - half][d - 1],
        )

    def z_copy(d):
        return remote(
            gall.at[head], gall.at[head],
            z_send.at[d - 1], z_recv.at[d - 1], z_peers[d - 1],
        )

    mine = [
        pl.ds(pl.multiple_of(x * XB + y * YB, YB), YB),
        pl.ds(pl.multiple_of(y * XB + x * YB, YB), YB),
    ]

    def first_copy(half, d):
        return remote(
            gv.at[half, mine[half]], gv.at[half, mine[half]],
            gy_send.at[half, d - 1], gy_recv.at[half, d - 1],
            (y_peers, x_peers)[half][d - 1],
        )

    def second_copy(half, d):
        rows = x_rows((x, y)[half])
        return remote(
            gv.at[half, rows], gv.at[half, rows],
            gx_send.at[half, d - 1], gx_recv.at[half, d - 1],
            (x_peers, y_peers)[half][d - 1],
        )

    for c in loads:
        c.start()
    barrier = pltpu.get_barrier_semaphore()
    for peer in everyone:
        pl.semaphore_signal(barrier, inc=1, device_id=peer, device_id_type=MESH)
    for i in range(NX):
        for j in range(NY):
            gk_turned[j * XB + i * YB:j * XB + (i + 1) * YB, :] = gk_ref[
                i * XB + j * YB:i * XB + (j + 1) * YB, SIDE:
            ]
    pl.semaphore_wait(barrier, len(everyone))
    send_halos(0)

    offset = (seq * TOK).astype(F32)
    span_first = as_column(span_ref[0:1, :], GLOB) - offset
    span_after = as_column(span_ref[1:2, :], GLOB) - offset
    lane_f = lax.broadcasted_iota(jnp.int32, (GLOB, 128), 1).astype(F32)

    @pl.loop(0, TOK // 128)
    def _(j):
        place = lane_f + (j * 128).astype(F32)
        bias[:, pl.ds(pl.multiple_of(j * 128, 128), 128)] = jnp.where(
            (place >= span_first) & (place < span_after), 0.0, EXCLUDED
        )

    loads[0].wait()
    loads[1].wait()
    lane = lax.broadcasted_iota(jnp.int32, (GLOB, 128), 1)
    stats = [jnp.zeros((GLOB, 128), F32)] * 2

    def put_rows(half, part, rows):
        if half == 0:
            msg[half, part] = rows
            return
        for i in range(NX):
            for j in range(NY):
                msg[half, part, j * XB + i * YB:j * XB + (i + 1) * YB, :] = rows[
                    i * XB + j * YB:i * XB + (j + 1) * YB
                ]

    for h in range(HERE):
        half, part_at = h // PAIR, h % PAIR
        cols = slice(h * HD, (h + 1) * HD)
        queries = scaled_parts(gq_ref[:, cols])
        score, weight = scores.at[h % 2], weights.at[h % 2]
        tops = []
        for c in range(0, TOK, TILE):
            part = dot_nt(queries, twice(kbuf[RADIUS + c:RADIUS + c + TILE, cols]))
            part = part + bias[:, c:c + TILE]
            score[:, c:c + TILE] = part
            tops.append(jnp.maximum(part[:, :128], part[:, 128:]))
        peak = jnp.max(functools.reduce(jnp.maximum, tops), axis=1, keepdims=True)
        for c in range(0, TOK, TILE):
            weight[:, c:c + TILE] = jnp.exp2(score[:, c:c + TILE] - peak).astype(BF16)
        acc = dot_nn(weight[...], with_ones(vbuf[own, cols]))
        put_rows(half, part_at, (acc[:, :HD] / acc[:, HD:]).astype(BF16))
        stats[half] = put_log(stats[half], part_at, peak + jnp.log2(acc[:, HD:]), lane)
    for half in range(2):
        put_rows(half, PAIR, stats[half].astype(BF16))
    for d in (2, 1, 3):
        for half in range(2):
            part_copy(half, d).start()
    loads[2].wait()

    def after_x():
        lane = lax.broadcasted_iota(jnp.int32, (XB, 128), 1)
        for half in range(2):
            for d in range(1, NX):
                part_copy(half, d).wait_recv()
        for half in range(2):
            mine = x_rows(block[half])
            parts = [[msg[half, h, mine, :] for h in range(PARTS)]]
            parts += [[msg_x[half, d, h] for h in range(PARTS)] for d in range(NX - 1)]
            outs, logs = combine(parts, XB)
            stat = jnp.zeros((XB, 128), F32)
            for h in range(PAIR):
                msg2[half, h] = outs[h].astype(BF16)
                stat = put_log(stat, h, logs[h], lane)
            msg2[half, PAIR] = stat.astype(BF16)
        for d in range(1, NY):
            for half in range(2):
                merge_copy(half, d).start()
        send_halos(1)

    def after_y():
        for half in range(2):
            for d in range(1, NY):
                merge_copy(half, d).wait_recv()
        merged = []
        for half in range(2):
            mine = y_rows(block[1 - half])
            parts = [[msg2[half, h, mine, :] for h in range(PARTS)]]
            parts += [[msg_y[half, d, h] for h in range(PARTS)] for d in range(NY - 1)]
            merged += combine(parts, YB)[0]
        gall[head] = jnp.concatenate([o.astype(BF16) for o in merged], axis=1)
        for d in range(1, NHEAD):
            z_copy(d).start()
        send_halos(2)

    def after_z():
        for d in range(1, NHEAD):
            z_copy(d).wait_recv()
        squares = jnp.zeros((YB, 1), F32)
        for g in range(NHEAD):
            wide = gall[g].astype(F32)
            squares = squares + jnp.sum(wide * wide, axis=1, keepdims=True)
        inverse = lax.rsqrt(squares / (NHEAD * WIDTH) + 1e-06)
        loads[3].wait()
        total = jnp.zeros((YB, WIDTH), F32)
        for g in range(NHEAD):
            normed = (gall[g].astype(F32) * inverse).astype(BF16)
            total = total + dot_nn(normed, proj[g * WIDTH:(g + 1) * WIDTH, :])
        for half in range(2):
            gv[half, mine[half], :] = total[:, half * SIDE:(half + 1) * SIDE].astype(BF16)
        for d in range(1, NY):
            for half in range(2):
                first_copy(half, d).start()
        send_halos(3)

    def after_gy():
        for half in range(2):
            for d in range(1, NX):
                first_copy(half, d).wait_recv()
            for d in range(1, NX):
                second_copy(half, d).start()
        send_halos(4)

    def place_bias(t, start, width):
        here = pl.ds(pl.multiple_of(t * TILE, TILE), TILE)
        base = (seq * TOK - RADIUS + start).astype(F32)
        shift = (t * TILE - start).astype(F32)
        row = lax.broadcasted_iota(jnp.int32, (TILE, 128), 0).astype(F32) + shift
        lane = lax.broadcasted_iota(jnp.int32, (TILE, 128), 1).astype(F32)
        first = jnp.maximum(as_column(doc_ref[0:1, here], TILE) - base, row)
        after = jnp.minimum(
            as_column(doc_ref[1:2, here], TILE) - base, row + (2 * RADIUS + 1)
        )
        for j in range(width // 128):
            place = lane + float(j * 128)
            local_bias[:, j * 128:(j + 1) * 128] = jnp.where(
                (place >= first) & (place < after), 0.0, EXCLUDED
            )

    def own_keys(t, start, width, slot):
        place_bias(t, start, width)
        here = pl.ds(pl.multiple_of(t * TILE, TILE), TILE)
        window = pl.ds(pl.multiple_of(start, TILE), width)
        for h in range(HERE):
            cols = slice(h * HD, (h + 1) * HD)
            queries = scaled_parts(qbuf[here, cols])
            score, weight = scores.at[h % 2, :TILE], weights.at[h % 2, :TILE]
            tops = []
            for c in range(0, width, TILE):
                rows = pl.ds(pl.multiple_of(start + c, TILE), TILE)
                part = dot_nt(queries, twice(kbuf[rows, cols])) + local_bias[:, c:c + TILE]
                score[:, c:c + TILE] = part
                tops.append(jnp.maximum(part[:, :128], part[:, 128:]))
            edge_keys = gk_ref[:, cols] if h < 2 else gk_turned[:, (h - 2) * HD:(h - 1) * HD]
            for c in range(0, GLOB, TILE):
                part = dot_nt(queries, twice(edge_keys[c:c + TILE]))
                score[:, width + c:width + c + TILE] = part
                tops.append(jnp.maximum(part[:, :128], part[:, 128:]))
            peak = jnp.max(functools.reduce(jnp.maximum, tops), axis=1, keepdims=True)
            for c in range(0, width, TILE):
                weight[:, c:c + TILE] = jnp.exp2(score[:, c:c + TILE] - peak).astype(BF16)
            for c in range(0, GLOB, TILE):
                edges[t, h, :, c:c + TILE] = jnp.exp2(
                    score[:, width + c:width + c + TILE] - peak
                ).astype(BF16)
            sums[t, h] = dot_nn(weight[:, :width], with_ones(vbuf[window, cols]))
            if slot is not None:
                factor[slot, h] = jnp.broadcast_to(peak, (TILE, HD))

    def halo_keys(t, start, width, slot):
        place_bias(t, start, width)
        here = pl.ds(pl.multiple_of(t * TILE, TILE), TILE)
        window = pl.ds(pl.multiple_of(start, TILE), width)
        for h in range(HERE):
            cols = slice(h * HD, (h + 1) * HD)
            queries = scaled_parts(qbuf[here, cols])
            near = dot_nt(queries, twice(kbuf[window, cols])) + local_bias[:, :width]
            peak = jnp.max(near, axis=1, keepdims=True)
            near_exp = jnp.exp2(near - peak).astype(BF16)
            more = dot_nn(near_exp, with_ones(vbuf[window, cols]))
            old = factor[slot, h]
            top = jnp.maximum(old, peak)
            down, added = jnp.exp2(old - top), jnp.exp2(peak - top)
            for c in (slice(0, HD), slice(HD, 2 * HD)):
                sums[t, h, :, c] = sums[t, h, :, c] * down + more[:, c] * added
            factor[slot, h] = down

    first_in = RADIUS // TILE
    last_in = TILES - first_in

    @pl.loop(first_in, last_in)
    def _(t):
        own_keys(t, t * TILE, SPAN, None)
        pl.when(t == first_in + 1)(after_x)
        pl.when(t == first_in + 2)(after_y)

    far, mid = RADIUS + TILE, RADIUS + 2 * TILE

    @pl.loop(0, 2)
    def _(i):
        t = 1 + i * (TILES - 3)
        own_keys(t, RADIUS + i * (TOK - mid), mid, i)
        pl.when(i == 0)(after_z)
        pl.when(i == 1)(after_gy)

    @pl.loop(0, 2)
    def _(i):
        own_keys(i * (TILES - 1), RADIUS + i * (TOK - far), far, 2 + i)

    for c in range(2 * PIECES):
        for copy in halo_pair(c):
            copy.wait_recv()

    @pl.loop(0, 2)
    def _(i):
        halo_keys(1 + i * (TILES - 3), TILE + i * (TOK + TILE), TILE, i)
        halo_keys(i * (TILES - 1), i * (TOK + RADIUS), RADIUS, 2 + i)

    for half in range(2):
        for d in range(1, NX):
            second_copy(half, d).wait_recv()

    def out_copy(t):
        here = pl.ds(pl.multiple_of(t * TILE, TILE), TILE)
        return pltpu.make_async_copy(obuf.at[here], out_hbm.at[here], out_sems.at[t])

    def finish(t, slot):
        here = pl.ds(pl.multiple_of(t * TILE, TILE), TILE)
        for h in range(HERE):
            cols = slice(h * HD, (h + 1) * HD)
            edge = dot_nn(edges[t, h], with_ones(gv[h // 2, :, (h % 2) * HD:(h % 2 + 1) * HD]))
            upper, lower = edge[:, :HD], edge[:, HD:]
            if slot is not None:
                upper, lower = upper * factor[slot, h], lower * factor[slot, h]
            upper, lower = upper + sums[t, h, :, :HD], lower + sums[t, h, :, HD:]
            obuf[here, cols] = (upper / lower).astype(BF16)
        out_copy(t).start()

    @pl.loop(first_in, last_in)
    def _(t):
        finish(t, None)

    @pl.loop(0, 2)
    def _(i):
        finish(1 + i * (TILES - 3), i)
        finish(i * (TILES - 1), 2 + i)

    for t in range(TILES):
        out_copy(t).wait()
    for d in range(1, NX):
        for half in range(2):
            part_copy(half, d).wait_send()
            merge_copy(half, d).wait_send()
            first_copy(half, d).wait_send()
            second_copy(half, d).wait_send()
    for d in range(1, NHEAD):
        z_copy(d).wait_send()
    for c in range(2 * PIECES):
        for copy in halo_pair(c):
            copy.wait_send()


def local(queries, keys, values, doc_bounds, global_queries, global_keys, global_span, global_proj):
    anyspec = pl.BlockSpec(memory_space=pl.ANY)
    vmem = pl.BlockSpec(memory_space=pltpu.VMEM)
    dma = pltpu.SemaphoreType.DMA
    return pl.pallas_call(
        kernel,
        out_shape=jax.ShapeDtypeStruct((TOK, WIDTH), BF16),
        in_specs=[vmem] * 4 + [anyspec] * 4,
        out_specs=anyspec,
        scratch_shapes=[
            pltpu.VMEM((TOK, WIDTH), BF16),
            pltpu.VMEM((TOK + 2 * RADIUS, WIDTH), BF16),
            pltpu.VMEM((TOK + 2 * RADIUS, WIDTH), BF16),
            pltpu.VMEM((NHEAD * WIDTH, WIDTH), BF16),
            pltpu.VMEM((GLOB, TOK), F32),
            pltpu.VMEM((TILE, SPAN), F32),
            pltpu.VMEM((TILES, HERE, TILE, 2 * HD), F32),
            pltpu.VMEM((TILES, HERE, TILE, GLOB), BF16),
            pltpu.VMEM((2 * RADIUS // TILE, HERE, TILE, HD), F32),
            pltpu.VMEM((TOK, WIDTH), BF16),
            pltpu.VMEM((2, GLOB, TOK), F32),
            pltpu.VMEM((2, GLOB, TOK), BF16),
            pltpu.VMEM((2, PARTS, GLOB, HD), BF16),
            pltpu.VMEM((2, NX - 1, PARTS, XB, HD), BF16),
            pltpu.VMEM((2, PARTS, XB, HD), BF16),
            pltpu.VMEM((2, NY - 1, PARTS, YB, HD), BF16),
            pltpu.VMEM((NHEAD, YB, WIDTH), BF16),
            pltpu.VMEM((2, GLOB, SIDE), BF16),
            pltpu.VMEM((GLOB, SIDE), BF16),
            dma((4,)), dma((TILES,)), dma((2, 2 * PIECES)), dma((2, 2 * PIECES)),
            dma((2, NX - 1)), dma((2, NX - 1)), dma((2, NY - 1)), dma((2, NY - 1)),
            dma((NHEAD - 1,)), dma((NHEAD - 1,)),
            dma((2, NY - 1)), dma((2, NY - 1)), dma((2, NX - 1)), dma((2, NX - 1)),
        ],
        compiler_params=pltpu.CompilerParams(
            collective_id=0, has_side_effects=True, vmem_limit_bytes=63 * 2**20
        ),
        name="attention",
    )(
        global_queries, global_keys, global_span, doc_bounds,
        queries, keys, values, global_proj,
    )


def solution(mesh):
    in_specs = (
        P("seq", "head"),
        P("seq", "head"),
        P("seq", "head"),
        P(None, "seq"),
        P(None, "head"),
        P(None, "head"),
        P(),
        P(None, "head"),
    )
    out_specs = P("seq", "head")
    return jax.shard_map(local, mesh=mesh, in_specs=in_specs, out_specs=out_specs, check_vma=False)
```

```python
import functools
import math

import jax
import jax.numpy as jnp
from jax import lax
from jax.experimental import pallas as pl
from jax.experimental.pallas import tpu as pltpu
from jax.sharding import PartitionSpec as P

HD = 128
RADIUS = 512
HERE = 4
TOK = 2048
GLOB = 512
WIDTH = HERE * HD
TILE = 256
SPAN = TILE + 2 * RADIUS
EXCLUDED = -1e30
LOG2_SCALE = math.log2(math.e) / math.sqrt(HD)
NX = 4
NY = 4
NHEAD = 8
XB = GLOB // NX
YB = XB // NY
PAIR = HERE // 2
PIECES = 4
PIECE = RADIUS // PIECES
HALO_PLAN = (2, 1, 3, 1, 1)
PARTS = PAIR + 1
SIDE = WIDTH // 2
MESH = pl.DeviceIdType.MESH
F32 = jnp.float32
BF16 = jnp.bfloat16


def dot_nt(a, b):
    return lax.dot_general(a, b, (((1,), (1,)), ((), ())), preferred_element_type=F32)


def dot_nn(a, b):
    return jnp.dot(a, b, preferred_element_type=F32)


def twice(k):
    return jnp.concatenate([k, k], axis=1)


def with_ones(v):
    return jnp.concatenate([v, jnp.ones_like(v)], axis=1)


def scaled_parts(q):
    scaled = q.astype(F32) * LOG2_SCALE
    high = scaled.astype(BF16)
    low = (scaled - high.astype(F32)).astype(BF16)
    return jnp.concatenate([high, low], axis=1)


def as_column(row, count):
    return jnp.transpose(jnp.broadcast_to(row.astype(F32), (128, count)))


def combine(parts, rows):
    lane = lax.broadcasted_iota(jnp.int32, (rows, 128), 1)
    stats = [p[PAIR].astype(F32) for p in parts]
    outs, logs = [], []
    for h in range(PAIR):
        mine = (lane >= 3 * h) & (lane < 3 * h + 3)
        lse = [jnp.sum(jnp.where(mine, s, 0.0), axis=1, keepdims=True) for s in stats]
        top = functools.reduce(jnp.maximum, lse)
        weights = [jnp.exp2(x - top) for x in lse]
        total = functools.reduce(jnp.add, weights)
        acc = functools.reduce(
            jnp.add, [w * p[h].astype(F32) for w, p in zip(weights, parts)]
        )
        outs.append(acc / total)
        logs.append(top + jnp.log2(total))
    return outs, logs


def put_log(stat, h, log, lane):
    high = log.astype(BF16).astype(F32)
    mid = (log - high).astype(BF16).astype(F32)
    low = log - high - mid
    stat = jnp.where(lane == 3 * h, high, stat)
    stat = jnp.where(lane == 3 * h + 1, mid, stat)
    return jnp.where(lane == 3 * h + 2, low, stat)


TILES = TOK // TILE


def kernel(
    gq_ref, gk_ref, span_ref, doc_ref, q_hbm, k_hbm, v_hbm, proj_hbm, out_hbm,
    qbuf, kbuf, vbuf, proj, bias, local_bias, sums, edges, factor, obuf, scores, weights,
    msg, msg_x, msg2, msg_y, gall, gv, gk_turned,
    load_sems, out_sems, halo_send, halo_recv, x_send, x_recv, y_send, y_recv,
    z_send, z_recv, gy_send, gy_recv, gx_send, gx_recv,
):
    seq = lax.axis_index("seq")
    head = lax.axis_index("head")
    x, y = seq // NY, seq % NY
    right = ((seq + 1) % (NX * NY), head)
    left = ((seq + NX * NY - 1) % (NX * NY), head)
    x_peers = [(((x + d) % NX) * NY + y, head) for d in range(1, NX)]
    y_peers = [(x * NY + (y + d) % NY, head) for d in range(1, NY)]
    z_peers = [(seq, (head + d) % NHEAD) for d in range(1, NHEAD)]
    everyone = [left, right] + x_peers + y_peers + z_peers

    def remote(src, dst, send, recv, peer):
        return pltpu.make_async_remote_copy(
            src_ref=src, dst_ref=dst, send_sem=send, recv_sem=recv,
            device_id=peer, device_id_type=MESH,
        )

    def x_rows(b):
        return pl.ds(pl.multiple_of(b * XB, XB), XB)

    def y_rows(b):
        return pl.ds(pl.multiple_of(b * YB, YB), YB)

    own = pl.ds(RADIUS, TOK)
    loads = [
        pltpu.make_async_copy(k_hbm, kbuf.at[own], load_sems.at[0]),
        pltpu.make_async_copy(v_hbm, vbuf.at[own], load_sems.at[1]),
        pltpu.make_async_copy(q_hbm, qbuf, load_sems.at[2]),
        pltpu.make_async_copy(proj_hbm, proj, load_sems.at[3]),
    ]
    def halo_pair(c):
        src, dst = (k_hbm, kbuf) if c < PIECES else (v_hbm, vbuf)
        at = (c % PIECES) * PIECE
        return [
            remote(
                src.at[pl.ds(TOK - RADIUS + at, PIECE)], dst.at[pl.ds(at, PIECE)],
                halo_send.at[0, c], halo_recv.at[0, c], right,
            ),
            remote(
                src.at[pl.ds(at, PIECE)], dst.at[pl.ds(TOK + RADIUS + at, PIECE)],
                halo_send.at[1, c], halo_recv.at[1, c], left,
            ),
        ]

    def send_halos(stage):
        first = sum(HALO_PLAN[:stage])
        for c in range(first, first + HALO_PLAN[stage]):
            for copy in halo_pair(c):
                copy.start()

    block = (x, y)
    line_peers = (x_peers, y_peers)

    def part_copy(half, d):
        return remote(
            msg.at[half, :, x_rows((block[half] + d) % NX)], msg_x.at[half, d - 1],
            x_send.at[half, d - 1], x_recv.at[half, d - 1], line_peers[half][d - 1],
        )

    def merge_copy(half, d):
        return remote(
            msg2.at[half, :, y_rows((block[1 - half] + d) % NY)], msg_y.at[half, d - 1],
            y_send.at[half, d - 1], y_recv.at[half, d - 1], line_peers[1 - half][d - 1],
        )

    def z_copy(d):
        return remote(
            gall.at[head], gall.at[head],
            z_send.at[d - 1], z_recv.at[d - 1], z_peers[d - 1],
        )

    mine = [
        pl.ds(pl.multiple_of(x * XB + y * YB, YB), YB),
        pl.ds(pl.multiple_of(y * XB + x * YB, YB), YB),
    ]

    def first_copy(half, d):
        return remote(
            gv.at[half, mine[half]], gv.at[half, mine[half]],
            gy_send.at[half, d - 1], gy_recv.at[half, d - 1],
            (y_peers, x_peers)[half][d - 1],
        )

    def second_copy(half, d):
        rows = x_rows((x, y)[half])
        return remote(
            gv.at[half, rows], gv.at[half, rows],
            gx_send.at[half, d - 1], gx_recv.at[half, d - 1],
            (x_peers, y_peers)[half][d - 1],
        )

    for c in loads:
        c.start()
    barrier = pltpu.get_barrier_semaphore()
    for peer in everyone:
        pl.semaphore_signal(barrier, inc=1, device_id=peer, device_id_type=MESH)
    for i in range(NX):
        for j in range(NY):
            gk_turned[j * XB + i * YB:j * XB + (i + 1) * YB, :] = gk_ref[
                i * XB + j * YB:i * XB + (j + 1) * YB, SIDE:
            ]
    pl.semaphore_wait(barrier, len(everyone))
    send_halos(0)

    offset = (seq * TOK).astype(F32)
    span_first = as_column(span_ref[0:1, :], GLOB) - offset
    span_after = as_column(span_ref[1:2, :], GLOB) - offset
    lane_f = lax.broadcasted_iota(jnp.int32, (GLOB, 128), 1).astype(F32)

    @pl.loop(0, TOK // 128)
    def _(j):
        place = lane_f + (j * 128).astype(F32)
        bias[:, pl.ds(pl.multiple_of(j * 128, 128), 128)] = jnp.where(
            (place >= span_first) & (place < span_after), 0.0, EXCLUDED
        )

    loads[0].wait()
    loads[1].wait()
    lane = lax.broadcasted_iota(jnp.int32, (GLOB, 128), 1)
    stats = [jnp.zeros((GLOB, 128), F32)] * 2

    def put_rows(half, part, rows):
        if half == 0:
            msg[half, part] = rows
            return
        for i in range(NX):
            for j in range(NY):
                msg[half, part, j * XB + i * YB:j * XB + (i + 1) * YB, :] = rows[
                    i * XB + j * YB:i * XB + (j + 1) * YB
                ]

    for h in range(HERE):
        half, part_at = h // PAIR, h % PAIR
        cols = slice(h * HD, (h + 1) * HD)
        queries = scaled_parts(gq_ref[:, cols])
        score, weight = scores.at[h % 2], weights.at[h % 2]
        tops = []
        for c in range(0, TOK, TILE):
            part = dot_nt(queries, twice(kbuf[RADIUS + c:RADIUS + c + TILE, cols]))
            part = part + bias[:, c:c + TILE]
            score[:, c:c + TILE] = part
            tops.append(jnp.maximum(part[:, :128], part[:, 128:]))
        peak = jnp.max(functools.reduce(jnp.maximum, tops), axis=1, keepdims=True)
        for c in range(0, TOK, TILE):
            weight[:, c:c + TILE] = jnp.exp2(score[:, c:c + TILE] - peak).astype(BF16)
        acc = dot_nn(weight[...], with_ones(vbuf[own, cols]))
        put_rows(half, part_at, (acc[:, :HD] / acc[:, HD:]).astype(BF16))
        stats[half] = put_log(stats[half], part_at, peak + jnp.log2(acc[:, HD:]), lane)
    for half in range(2):
        put_rows(half, PAIR, stats[half].astype(BF16))
    for d in (2, 1, 3):
        for half in range(2):
            part_copy(half, d).start()
    loads[2].wait()

    def after_x():
        lane = lax.broadcasted_iota(jnp.int32, (XB, 128), 1)
        for half in range(2):
            for d in range(1, NX):
                part_copy(half, d).wait_recv()
        for half in range(2):
            mine = x_rows(block[half])
            parts = [[msg[half, h, mine, :] for h in range(PARTS)]]
            parts += [[msg_x[half, d, h] for h in range(PARTS)] for d in range(NX - 1)]
            outs, logs = combine(parts, XB)
            stat = jnp.zeros((XB, 128), F32)
            for h in range(PAIR):
                msg2[half, h] = outs[h].astype(BF16)
                stat = put_log(stat, h, logs[h], lane)
            msg2[half, PAIR] = stat.astype(BF16)
        for d in range(1, NY):
            for half in range(2):
                merge_copy(half, d).start()
        send_halos(1)

    def after_y():
        for half in range(2):
            for d in range(1, NY):
                merge_copy(half, d).wait_recv()
        merged = []
        for half in range(2):
            mine = y_rows(block[1 - half])
            parts = [[msg2[half, h, mine, :] for h in range(PARTS)]]
            parts += [[msg_y[half, d, h] for h in range(PARTS)] for d in range(NY - 1)]
            merged += combine(parts, YB)[0]
        gall[head] = jnp.concatenate([o.astype(BF16) for o in merged], axis=1)
        for d in range(1, NHEAD):
            z_copy(d).start()
        send_halos(2)

    def after_z():
        for d in range(1, NHEAD):
            z_copy(d).wait_recv()
        squares = jnp.zeros((YB, 1), F32)
        for g in range(NHEAD):
            wide = gall[g].astype(F32)
            squares = squares + jnp.sum(wide * wide, axis=1, keepdims=True)
        inverse = lax.rsqrt(squares / (NHEAD * WIDTH) + 1e-06)
        loads[3].wait()
        total = jnp.zeros((YB, WIDTH), F32)
        for g in range(NHEAD):
            normed = (gall[g].astype(F32) * inverse).astype(BF16)
            total = total + dot_nn(normed, proj[g * WIDTH:(g + 1) * WIDTH, :])
        for half in range(2):
            gv[half, mine[half], :] = total[:, half * SIDE:(half + 1) * SIDE].astype(BF16)
        for d in range(1, NY):
            for half in range(2):
                first_copy(half, d).start()
        send_halos(3)

    def after_gy():
        for half in range(2):
            for d in range(1, NX):
                first_copy(half, d).wait_recv()
            for d in range(1, NX):
                second_copy(half, d).start()
        send_halos(4)

    def place_bias(t, start, width):
        here = pl.ds(pl.multiple_of(t * TILE, TILE), TILE)
        base = (seq * TOK - RADIUS + start).astype(F32)
        shift = (t * TILE - start).astype(F32)
        row = lax.broadcasted_iota(jnp.int32, (TILE, 128), 0).astype(F32) + shift
        lane = lax.broadcasted_iota(jnp.int32, (TILE, 128), 1).astype(F32)
        first = jnp.maximum(as_column(doc_ref[0:1, here], TILE) - base, row)
        after = jnp.minimum(
            as_column(doc_ref[1:2, here], TILE) - base, row + (2 * RADIUS + 1)
        )
        for j in range(width // 128):
            place = lane + float(j * 128)
            local_bias[:, j * 128:(j + 1) * 128] = jnp.where(
                (place >= first) & (place < after), 0.0, EXCLUDED
            )

    def own_keys(t, start, width, slot):
        place_bias(t, start, width)
        here = pl.ds(pl.multiple_of(t * TILE, TILE), TILE)
        window = pl.ds(pl.multiple_of(start, TILE), width)
        for h in range(HERE):
            cols = slice(h * HD, (h + 1) * HD)
            queries = scaled_parts(qbuf[here, cols])
            score, weight = scores.at[h % 2, :TILE], weights.at[h % 2, :TILE]
            tops = []
            for c in range(0, width, TILE):
                rows = pl.ds(pl.multiple_of(start + c, TILE), TILE)
                part = dot_nt(queries, twice(kbuf[rows, cols])) + local_bias[:, c:c + TILE]
                score[:, c:c + TILE] = part
                tops.append(jnp.maximum(part[:, :128], part[:, 128:]))
            edge_keys = gk_ref[:, cols] if h < 2 else gk_turned[:, (h - 2) * HD:(h - 1) * HD]
            for c in range(0, GLOB, TILE):
                part = dot_nt(queries, twice(edge_keys[c:c + TILE]))
                score[:, width + c:width + c + TILE] = part
                tops.append(jnp.maximum(part[:, :128], part[:, 128:]))
            peak = jnp.max(functools.reduce(jnp.maximum, tops), axis=1, keepdims=True)
            for c in range(0, width, TILE):
                weight[:, c:c + TILE] = jnp.exp2(score[:, c:c + TILE] - peak).astype(BF16)
            for c in range(0, GLOB, TILE):
                edges[t, h, :, c:c + TILE] = jnp.exp2(
                    score[:, width + c:width + c + TILE] - peak
                ).astype(BF16)
            sums[t, h] = dot_nn(weight[:, :width], with_ones(vbuf[window, cols]))
            if slot is not None:
                factor[slot, h] = jnp.broadcast_to(peak, (TILE, HD))

    def halo_keys(t, start, width, slot):
        place_bias(t, start, width)
        here = pl.ds(pl.multiple_of(t * TILE, TILE), TILE)
        window = pl.ds(pl.multiple_of(start, TILE), width)
        for h in range(HERE):
            cols = slice(h * HD, (h + 1) * HD)
            queries = scaled_parts(qbuf[here, cols])
            near = dot_nt(queries, twice(kbuf[window, cols])) + local_bias[:, :width]
            peak = jnp.max(near, axis=1, keepdims=True)
            near_exp = jnp.exp2(near - peak).astype(BF16)
            more = dot_nn(near_exp, with_ones(vbuf[window, cols]))
            old = factor[slot, h]
            top = jnp.maximum(old, peak)
            down, added = jnp.exp2(old - top), jnp.exp2(peak - top)
            for c in (slice(0, HD), slice(HD, 2 * HD)):
                sums[t, h, :, c] = sums[t, h, :, c] * down + more[:, c] * added
            factor[slot, h] = down

    first_in = RADIUS // TILE
    last_in = TILES - first_in

    @pl.loop(first_in, last_in)
    def _(t):
        own_keys(t, t * TILE, SPAN, None)
        pl.when(t == first_in + 1)(after_x)
        pl.when(t == first_in + 2)(after_y)

    far, mid = RADIUS + TILE, RADIUS + 2 * TILE

    @pl.loop(0, 2)
    def _(i):
        t = 1 + i * (TILES - 3)
        own_keys(t, RADIUS + i * (TOK - mid), mid, i)
        pl.when(i == 0)(after_z)
        pl.when(i == 1)(after_gy)

    @pl.loop(0, 2)
    def _(i):
        own_keys(i * (TILES - 1), RADIUS + i * (TOK - far), far, 2 + i)

    for half in range(2):
        for d in range(1, NX):
            second_copy(half, d).wait_recv()

    def out_copy(t):
        here = pl.ds(pl.multiple_of(t * TILE, TILE), TILE)
        return pltpu.make_async_copy(obuf.at[here], out_hbm.at[here], out_sems.at[t])

    def finish(t, slot):
        here = pl.ds(pl.multiple_of(t * TILE, TILE), TILE)
        for h in range(HERE):
            cols = slice(h * HD, (h + 1) * HD)
            edge = dot_nn(edges[t, h], with_ones(gv[h // 2, :, (h % 2) * HD:(h % 2 + 1) * HD]))
            upper, lower = edge[:, :HD], edge[:, HD:]
            if slot is not None:
                upper, lower = upper * factor[slot, h], lower * factor[slot, h]
            upper, lower = upper + sums[t, h, :, :HD], lower + sums[t, h, :, HD:]
            obuf[here, cols] = (upper / lower).astype(BF16)
        out_copy(t).start()

    @pl.loop(first_in, last_in)
    def _(t):
        finish(t, None)

    for c in range(2 * PIECES):
        for copy in halo_pair(c):
            copy.wait_recv()

    @pl.loop(0, 2)
    def _(i):
        halo_keys(1 + i * (TILES - 3), TILE + i * (TOK + TILE), TILE, i)
        halo_keys(i * (TILES - 1), i * (TOK + RADIUS), RADIUS, 2 + i)

    @pl.loop(0, 2)
    def _(i):
        finish(1 + i * (TILES - 3), i)
        finish(i * (TILES - 1), 2 + i)

    for t in range(TILES):
        out_copy(t).wait()
    for d in range(1, NX):
        for half in range(2):
            part_copy(half, d).wait_send()
            merge_copy(half, d).wait_send()
            first_copy(half, d).wait_send()
            second_copy(half, d).wait_send()
    for d in range(1, NHEAD):
        z_copy(d).wait_send()
    for c in range(2 * PIECES):
        for copy in halo_pair(c):
            copy.wait_send()


def local(queries, keys, values, doc_bounds, global_queries, global_keys, global_span, global_proj):
    anyspec = pl.BlockSpec(memory_space=pl.ANY)
    vmem = pl.BlockSpec(memory_space=pltpu.VMEM)
    dma = pltpu.SemaphoreType.DMA
    return pl.pallas_call(
        kernel,
        out_shape=jax.ShapeDtypeStruct((TOK, WIDTH), BF16),
        in_specs=[vmem] * 4 + [anyspec] * 4,
        out_specs=anyspec,
        scratch_shapes=[
            pltpu.VMEM((TOK, WIDTH), BF16),
            pltpu.VMEM((TOK + 2 * RADIUS, WIDTH), BF16),
            pltpu.VMEM((TOK + 2 * RADIUS, WIDTH), BF16),
            pltpu.VMEM((NHEAD * WIDTH, WIDTH), BF16),
            pltpu.VMEM((GLOB, TOK), F32),
            pltpu.VMEM((TILE, SPAN), F32),
            pltpu.VMEM((TILES, HERE, TILE, 2 * HD), F32),
            pltpu.VMEM((TILES, HERE, TILE, GLOB), BF16),
            pltpu.VMEM((2 * RADIUS // TILE, HERE, TILE, HD), F32),
            pltpu.VMEM((TOK, WIDTH), BF16),
            pltpu.VMEM((2, GLOB, TOK), F32),
            pltpu.VMEM((2, GLOB, TOK), BF16),
            pltpu.VMEM((2, PARTS, GLOB, HD), BF16),
            pltpu.VMEM((2, NX - 1, PARTS, XB, HD), BF16),
            pltpu.VMEM((2, PARTS, XB, HD), BF16),
            pltpu.VMEM((2, NY - 1, PARTS, YB, HD), BF16),
            pltpu.VMEM((NHEAD, YB, WIDTH), BF16),
            pltpu.VMEM((2, GLOB, SIDE), BF16),
            pltpu.VMEM((GLOB, SIDE), BF16),
            dma((4,)), dma((TILES,)), dma((2, 2 * PIECES)), dma((2, 2 * PIECES)),
            dma((2, NX - 1)), dma((2, NX - 1)), dma((2, NY - 1)), dma((2, NY - 1)),
            dma((NHEAD - 1,)), dma((NHEAD - 1,)),
            dma((2, NY - 1)), dma((2, NY - 1)), dma((2, NX - 1)), dma((2, NX - 1)),
        ],
        compiler_params=pltpu.CompilerParams(
            collective_id=0, has_side_effects=True, vmem_limit_bytes=63 * 2**20
        ),
        name="attention",
    )(
        global_queries, global_keys, global_span, doc_bounds,
        queries, keys, values, global_proj,
    )


def solution(mesh):
    in_specs = (
        P("seq", "head"),
        P("seq", "head"),
        P("seq", "head"),
        P(None, "seq"),
        P(None, "head"),
        P(None, "head"),
        P(),
        P(None, "head"),
    )
    out_specs = P("seq", "head")
    return jax.shard_map(local, mesh=mesh, in_specs=in_specs, out_specs=out_specs, check_vma=False)
```
